32 devices in a mesh: segment: 2 (over x), expert: 16 (over z, y, core).
Axes of the slice: x: 2, y: 2, z: 4, core: 2. Of those that a mesh axis runs over, the one named last changes fastest.
Arguments:
- boundary: bfloat16 [2, 1024, 2048], P('segment', 'expert'), may hold values from -6 to 6
- saved: bfloat16 [2, 1024, 2048], P('segment', 'expert'), may hold values from -6 to 6
- norm_gain: float32 [2, 2048], P('segment'), may hold values from 0.25 to 1.75
- gate_weight: bfloat16 [2, 16, 2048, 768], P('segment', 'expert'), may hold values from -0.125 to 0.125
- up_weight: bfloat16 [2, 16, 2048, 768], P('segment', 'expert'), may hold values from -0.125 to 0.125
- down_weight: bfloat16 [2, 16, 768, 2048], P('segment', 'expert'), may hold values from -0.21875 to 0.21875
- routes: int32 [2, 2, 1024, 8], P('segment', None, 'expert'), may hold values from 0 to 15, all different within a row; in each aligned block of 64 rows (0 to 63, 64 to 127, ..., all dimensions but the last counted through in order) at most 48 rows name the same one
- gate_codes: int32 [2, 2, 1024, 8], P('segment', None, 'expert'), may hold values from 1 to 16
Outputs:
- results: bfloat16 [2, 1024, 2048], P('segment', 'expert')
The draws below stay inside these ranges and needn't reach their ends.
Inputs may be any that keep to these rules, and one draw needn't show every extreme that they name: `routes`: each row names 8 different experts. Among the rows of one index of expert (aligned blocks of 64 rows) no expert is named by more than 48 rows, a bound that some block reaches.
All inputs are finite; a program needn't handle non-finite values.
Results may differ from the reference program's by a relative error of at most 0.0075.
Values may be sent and summed in bfloat16 or wider, within the bound.
A program may use at most 128 MiB of HBM per device.

```python
import math
import jax
import jax.numpy as jnp
import numpy as np
from jax import lax

D = 2048
FF = 768
TOP = 8
EXPERTS = 16
TOK_DEV = 64
TOKENS = 1024
CAP = 48
N_EXPERT = 16


def set_ends(drawn, rng, least, largest):
    index_at = [jax.random.randint(jax.random.fold_in(rng, axis), (), 0, length) for axis, length in enumerate(drawn.shape)]
    main_axis = drawn.shape.index(max(drawn.shape))
    beside = index_at[:main_axis] + [(index_at[main_axis] + 1) % drawn.shape[main_axis]] + index_at[main_axis + 1:]
    return drawn.at[tuple(index_at)].set(least).at[tuple(beside)].set(largest)


def block_levels(own_key, dims, cuts, smallest, largest):
    factor_of, own = 1.0, jax.random.fold_in(own_key, 6)
    for axis_at, shards_of in cuts:
        heights = jnp.exp(jax.random.uniform(jax.random.fold_in(own, axis_at), (shards_of,), jnp.float32, smallest / len(cuts), largest / len(cuts)))
        factor_of = factor_of * jnp.repeat(heights, dims[axis_at] // shards_of).reshape([-1 if axis == axis_at else 1 for axis in range(len(dims))])
    return factor_of


def assign_block(stream_key, own, number, rows, number_of, top, limit, skew):
    sequence = jax.random.permutation(stream_key, number_of)
    heavy_load, common = shares(number_of, rows * top, limit, skew, True), shares(number_of, rows * top, limit, skew, False)
    places = jnp.arange(number_of)

    def named(tallies, turn):
        used = int((tallies > 0).sum())
        fixed = max(1, used // 4)
        moved = fixed + (places - fixed + turn * (used - fixed)) % max(1, number_of - fixed)
        return jnp.zeros((number_of,), jnp.int32).at[sequence[jnp.where(places < fixed, places, moved)]].set(jnp.asarray(tallies, jnp.int32))

    tallies = jnp.where(number % 4 == 0, named(heavy_load, number // 4), named(common, number - number // 4 - 1))
    mixed = jax.random.permutation(jax.random.fold_in(own, 3), number_of)
    source_of, taker = mixed[0:number_of // 2 * 2:2], mixed[1:number_of // 2 * 2:2]
    room = jnp.minimum(tallies[source_of] - 1, limit - tallies[taker]) // 2
    room = jnp.where((source_of == sequence[0]) | (taker == sequence[0]) | (tallies[taker] == 0), 0, jnp.maximum(room, 0))
    moved = jax.random.randint(jax.random.fold_in(own, 4), (number_of // 2,), 0, 1 << 20) % (room + 1)
    tallies = tallies.at[source_of].add(-moved).at[taker].add(moved)
    members = jnp.searchsorted(jnp.cumsum(tallies), jnp.arange(rows * top), side="right").astype(jnp.int32)
    grid = members.reshape(top, rows).T
    grid = grid[jax.random.permutation(jax.random.fold_in(own, 1), rows)]
    turn = jax.random.randint(jax.random.fold_in(own, 2), (rows, 1), 0, top)
    return jnp.take_along_axis(grid, (jnp.arange(top)[None, :] + turn) % top, axis=1)


def shares(count, total, most, skew, full):
    portions = [(1 << 20) // math.isqrt(standing ** skew) + 1 for standing in range(1, count + 1)]
    largest = most if full else min(most, max(-(-total // count), total * portions[0] // sum(portions)))
    least = 1 if total - largest >= count - 1 else 0
    counts, surplus = [largest] + [least] * (count - 1), total - largest - least * (count - 1)
    while surplus > 0:
        movable = [i for i in range(1, count) if counts[i] < largest] or [i for i in range(1, count) if counts[i] < most]
        whole, remaining = sum([portions[i] for i in movable]), surplus
        for i in movable:
            extra = min(most - counts[i], max(1, remaining * portions[i] // whole), surplus)
            counts[i] = counts[i] + extra
            surplus = surplus - extra
    return np.array(counts)


def centred(key, extent, width, limit, split=(), held_as=jnp.bfloat16):
    factor_of = block_levels(key, extent, split, -0.22, 0.18) if split else 1.0
    result = jax.random.normal(key, extent, jnp.float32) * width * factor_of
    return jnp.minimum(jnp.maximum(result, -limit), limit).astype(held_as)


def setup_inputs(seed: int = 0) -> dict:
    streams_of = jax.random.split(jax.random.key(seed), 9)
    boundary = centred(streams_of[0], (2, TOKENS, D), 1.0, 6.0, ((0, 2), (1, 16)))
    saved = centred(streams_of[1], (2, TOKENS, D), 1.0, 6.0, ((0, 2), (1, 16)))
    norm_gain = jnp.clip(1.0 + 0.15 * jax.random.normal(streams_of[2], (2, D), jnp.float32), 0.25, 1.75)
    gate_weight = centred(streams_of[3], (2, EXPERTS, D, FF), D ** -0.5, 0.125, ((0, 2), (1, 16)))
    up_weight = centred(streams_of[4], (2, EXPERTS, D, FF), D ** -0.5, 0.125, ((0, 2), (1, 16)))
    down_weight = centred(streams_of[5], (2, EXPERTS, FF, D), FF ** -0.5, 0.21875, ((0, 2), (1, 16)))
    routes_keys = jax.random.split(jax.random.fold_in(streams_of[6], 1), 2 * 2 * TOKENS // TOK_DEV)
    routes_turns = jax.random.permutation(jax.random.fold_in(streams_of[6], 3), 2 * 2 * TOKENS // TOK_DEV)
    routes = jax.vmap(lambda own, number: assign_block(jax.random.fold_in(streams_of[6], 2), own, number, TOK_DEV, EXPERTS, TOP, CAP, 2))(routes_keys, routes_turns).reshape((2, 2, TOKENS, TOP))
    gate_codes = set_ends(jax.random.randint(streams_of[7], (2, 2, TOKENS, TOP), 1, 17), jax.random.fold_in(streams_of[7], 1), 1, 16).astype(jnp.int32)
    return dict(boundary=boundary, saved=saved, norm_gain=norm_gain, gate_weight=gate_weight, up_weight=up_weight, down_weight=down_weight, routes=routes, gate_codes=gate_codes)


epsilon = 1e-06

def gate_values(codes):
    counted = codes.astype(jnp.float32)
    return counted / lax.optimization_barrier(jnp.sum(counted, axis=-1, keepdims=True))

def normalize(inputs, gain_row):
    widened = inputs.astype(jnp.float32)
    scaling = lax.rsqrt(lax.optimization_barrier(jnp.mean(widened * widened, axis=-1, keepdims=True)) + epsilon)
    return (widened, scaling, (widened * scaling * gain_row).astype(jnp.bfloat16))

def transposed(left, right):
    return lax.dot_general(left, right, (((1,), (1,)), ((), ())), preferred_element_type=jnp.float32)

def expert_forward(row_block, w_gate, w_up, w_down):
    gate_part = jnp.dot(row_block, w_gate, preferred_element_type=jnp.float32)
    up_part = jnp.dot(row_block, w_up, preferred_element_type=jnp.float32)
    hidden = (gate_part * jax.nn.sigmoid(gate_part) * up_part).astype(jnp.bfloat16)
    return jnp.dot(hidden, w_down, preferred_element_type=jnp.float32).astype(jnp.bfloat16)

def expert_backward(row_block, grad_block, w_gate, w_up, w_down):
    gate_part = jnp.dot(row_block, w_gate, preferred_element_type=jnp.float32)
    up_part = jnp.dot(row_block, w_up, preferred_element_type=jnp.float32)
    sigmoid_part = jax.nn.sigmoid(gate_part)
    activated = gate_part * sigmoid_part
    slope = sigmoid_part * (1.0 + gate_part * (1.0 - sigmoid_part))
    hidden_grad = transposed(grad_block, w_down)
    gate_grad = (hidden_grad * up_part * slope).astype(jnp.bfloat16)
    up_grad = (hidden_grad * activated).astype(jnp.bfloat16)
    return (transposed(gate_grad, w_gate) + transposed(up_grad, w_up)).astype(jnp.bfloat16)

def expert_sums(route, gates, operands, weights, kernel):
    flat_ids = route.reshape(-1).astype(jnp.int32)
    assign_count = TOKENS * TOP
    slot_count = N_EXPERT * CAP
    assign_ids = jnp.arange(assign_count, dtype=jnp.int32)

    def one_expert(packed):
        expert_id, w_gate, w_up, w_down = packed
        matched = flat_ids == expert_id
        position = jnp.cumsum(matched.astype(jnp.int32)) - 1
        target = jnp.where(matched, position, slot_count).astype(jnp.int32)
        taken_ids = jnp.full((slot_count,), assign_count, jnp.int32).at[target].set(assign_ids, mode='drop')
        token_ids = jnp.minimum(taken_ids // TOP, TOKENS - 1).astype(jnp.int32)
        blocks = [jnp.take(operand, token_ids, axis=0) for operand in operands]
        if len(blocks) == 1:
            outputs = kernel(blocks[0], w_gate, w_up, w_down)
        else:
            outputs = kernel(blocks[0], blocks[1], w_gate, w_up, w_down)
        return (taken_ids, outputs)
    expert_ids = jnp.arange(N_EXPERT, dtype=jnp.int32)
    taken_all, outputs_all = lax.map(one_expert, (expert_ids, weights[0], weights[1], weights[2]))
    assigned = jnp.zeros((assign_count + 1, D), jnp.bfloat16)
    assigned = assigned.at[taken_all.reshape(-1)].set(outputs_all.reshape(-1, D))
    assigned = assigned[:assign_count].reshape(TOKENS, TOP, D)
    return jnp.einsum('tk,tkd->td', gates, assigned.astype(jnp.float32))

def layer_forward(inputs, gain_row, weights, route, codes):
    widened, scaling, normed = normalize(inputs, gain_row)
    summed = expert_sums(route, gate_values(codes), (normed,), weights, expert_forward)
    return (widened + summed).astype(jnp.bfloat16)

def layer_backward(inputs, upstream, gain_row, weights, route, codes):
    widened, scaling, normed = normalize(inputs, gain_row)
    summed = expert_sums(route, gate_values(codes), (normed, upstream), weights, expert_backward)
    scaled = summed * gain_row
    inner_mean = lax.optimization_barrier(jnp.mean(scaled * widened, axis=-1, keepdims=True))
    cubed = scaling * scaling * scaling
    return (upstream.astype(jnp.float32) + scaling * scaled - widened * cubed * inner_mean).astype(jnp.bfloat16)

def reference(boundary, saved, norm_gain, gate_weight, up_weight, down_weight, routes, gate_codes):
    first_weights = (gate_weight[0], up_weight[0], down_weight[0])
    second_weights = (gate_weight[1], up_weight[1], down_weight[1])
    hidden = layer_forward(boundary[0], norm_gain[0], first_weights, routes[0, 0], gate_codes[0, 0])
    grad_mid = layer_backward(saved[1], boundary[1], norm_gain[1], second_weights, routes[1, 1], gate_codes[1, 1])
    first_out = layer_backward(saved[0], grad_mid, norm_gain[0], first_weights, routes[0, 1], gate_codes[0, 1])
    second_out = layer_forward(hidden, norm_gain[1], second_weights, routes[1, 0], gate_codes[1, 0])
    return jnp.stack([first_out, second_out])
```

```python
import functools

import jax
import jax.numpy as jnp
from jax import lax
from jax.experimental import pallas as pl
from jax.experimental.pallas import tpu as pltpu
from jax.sharding import PartitionSpec as P

epsilon = 1e-06


def shifted(block, axis, distance):
    devices = range(lax.axis_size(axis))
    route = [(i - distance, i) for i in devices if i - distance in devices]
    return lax.ppermute(block, axis, route)


def gate_values(codes):
    counted = codes.astype(jnp.float32)
    return counted / jnp.sum(counted, axis=-1, keepdims=True)


def normalize(inputs, gain_row):
    widened = inputs.astype(jnp.float32)
    scaling = lax.rsqrt(jnp.mean(widened * widened, axis=-1, keepdims=True) + epsilon)
    return (widened, scaling, (widened * scaling * gain_row).astype(jnp.bfloat16))


def transposed(left, right):
    return lax.dot_general(
        left, right, (((1,), (1,)), ((), ())), preferred_element_type=jnp.float32
    )


def expert_forward(row_block, w_gate, w_up, w_down):
    gate_part = jnp.dot(row_block, w_gate, preferred_element_type=jnp.float32)
    up_part = jnp.dot(row_block, w_up, preferred_element_type=jnp.float32)
    hidden = (gate_part * jax.nn.sigmoid(gate_part) * up_part).astype(jnp.bfloat16)
    return jnp.dot(hidden, w_down, preferred_element_type=jnp.float32).astype(jnp.bfloat16)


def expert_backward(row_block, grad_block, w_gate, w_up, w_down):
    gate_part = jnp.dot(row_block, w_gate, preferred_element_type=jnp.float32)
    up_part = jnp.dot(row_block, w_up, preferred_element_type=jnp.float32)
    sigmoid_part = jax.nn.sigmoid(gate_part)
    activated = gate_part * sigmoid_part
    slope = sigmoid_part * (1.0 + gate_part * (1.0 - sigmoid_part))
    hidden_grad = transposed(grad_block, w_down)
    gate_grad = (hidden_grad * up_part * slope).astype(jnp.bfloat16)
    up_grad = (hidden_grad * activated).astype(jnp.bfloat16)
    return (transposed(gate_grad, w_gate) + transposed(up_grad, w_up)).astype(jnp.bfloat16)


def layout(route, codes, n_peer, capacity):
    tokens, top_count = route.shape
    flat_ids = route.reshape(-1)
    onehot = (flat_ids[:, None] == jnp.arange(n_peer, dtype=jnp.int32)[None, :]).astype(jnp.int32)
    spots = jnp.arange(flat_ids.shape[0], dtype=jnp.int32)
    earlier = (spots[None, :] < spots[:, None]).astype(jnp.bfloat16)
    before = jnp.dot(earlier, onehot.astype(jnp.bfloat16), preferred_element_type=jnp.float32)
    rank_in = jnp.sum(before.astype(jnp.int32) * onehot, axis=1)
    slot_of = flat_ids * capacity + rank_in
    slot_ids = jnp.arange(n_peer * capacity, dtype=jnp.int32)
    slot_hit = (slot_ids[:, None, None] == slot_of.reshape(tokens, top_count)[None, :, :]).astype(
        jnp.bfloat16
    )
    placing = jnp.sum(slot_hit, axis=2, dtype=jnp.float32).astype(jnp.bfloat16)
    return (placing, slot_of, gate_values(codes))


def dispatch(placing, payload, n_peer, capacity):
    picked = jnp.dot(placing, payload, preferred_element_type=jnp.float32).astype(jnp.bfloat16)
    return picked.reshape(n_peer, capacity, payload.shape[-1])


def collect(slot_of, gates, came_back):
    flat_rows = came_back.reshape(-1, came_back.shape[-1])
    chosen = jnp.take(flat_rows, slot_of, axis=0).reshape(
        gates.shape[0], gates.shape[1], flat_rows.shape[-1]
    )
    return jnp.einsum("tk,tkd->td", gates, chosen.astype(jnp.float32))


def apply_expert(forward_flag, first_rows, second_rows, weights):
    layout_of = first_rows.shape
    row_block = first_rows.reshape(-1, layout_of[-1])
    grad_block = second_rows.reshape(-1, layout_of[-1])
    outcome = lax.cond(
        forward_flag,
        lambda: expert_forward(row_block, weights[0], weights[1], weights[2]),
        lambda: expert_backward(row_block, grad_block, weights[0], weights[1], weights[2]),
    )
    return outcome.reshape(layout_of)


def return_rows(outcome):
    return lax.all_to_all(outcome, "expert", split_axis=0, concat_axis=0, tiled=True)


def finish(widened, scaling, gain_row, upstream, summed, forward_flag):
    forward_out = widened + summed
    scaled = summed * gain_row
    inner_mean = jnp.mean(scaled * widened, axis=-1, keepdims=True)
    cubed = scaling * scaling * scaling
    backward_out = upstream.astype(jnp.float32) + scaling * scaled - widened * cubed * inner_mean
    return jnp.where(forward_flag, forward_out, backward_out).astype(jnp.bfloat16)


def routed_body(boundary, saved, norm_gain, gate_weight, up_weight, down_weight, routes, gate_codes):
    first_segment = lax.axis_index("segment") == 0
    later_forward = jnp.logical_not(first_segment)
    n_peer = lax.axis_size("expert")
    tokens = boundary.shape[1]
    top_count = routes.shape[3]
    capacity = max(2, 3 * tokens * top_count // (2 * n_peer))
    weights = (gate_weight[0, 0], up_weight[0, 0], down_weight[0, 0])
    gain_row = norm_gain[0]
    edge_rows = boundary[0]
    stored = saved[0]
    route_now = jnp.where(first_segment, routes[0, 0], routes[0, 1])
    codes_now = jnp.where(first_segment, gate_codes[0, 0], gate_codes[0, 1])
    route_next = jnp.where(first_segment, routes[0, 1], routes[0, 0])
    codes_next = jnp.where(first_segment, gate_codes[0, 1], gate_codes[0, 0])
    place_now, slots_now, gates_now = layout(route_now, codes_now, n_peer, capacity)
    place_next, slots_next, gates_next = layout(route_next, codes_next, n_peer, capacity)
    inputs_now = jnp.where(first_segment, edge_rows, stored)
    widened, scaling, normed = normalize(inputs_now, gain_row)
    stored_normed = normalize(stored, gain_row)[2]
    early_rows = jnp.where(first_segment, stored_normed, edge_rows)
    early_place = jnp.where(first_segment, place_next, place_now)
    outgoing = (
        dispatch(place_now, normed, n_peer, capacity),
        dispatch(early_place, early_rows, n_peer, capacity),
    )
    paired = (
        lax.all_to_all(outgoing[0], "expert", split_axis=0, concat_axis=0, tiled=True),
        lax.all_to_all(outgoing[1], "expert", split_axis=0, concat_axis=0, tiled=True),
    )
    outcome = apply_expert(first_segment, paired[0], paired[1], weights)
    came_back = return_rows(outcome)
    kept_rows = paired[1]
    produced = finish(
        widened,
        scaling,
        gain_row,
        edge_rows,
        collect(slots_now, gates_now, came_back),
        first_segment,
    )
    arrived = shifted(produced, "segment", 1) + shifted(produced, "segment", -1)
    inputs_next = jnp.where(first_segment, stored, arrived)
    widened_next, scaling_next, normed_next = normalize(inputs_next, gain_row)
    member = jnp.where(first_segment, arrived, normed_next)
    landed = lax.all_to_all(
        dispatch(place_next, member, n_peer, capacity),
        "expert",
        split_axis=0,
        concat_axis=0,
        tiled=True,
    )
    outcome = apply_expert(
        later_forward, jnp.where(first_segment, kept_rows, landed), landed, weights
    )
    came_next = return_rows(outcome)
    result = finish(
        widened_next,
        scaling_next,
        gain_row,
        arrived,
        collect(slots_next, gates_next, came_next),
        later_forward,
    )
    return result[None]


def coefficients(route, codes, n_peer):
    hit = route[:, :, None] == jnp.arange(n_peer, dtype=jnp.int32)[None, None, :]
    return jnp.sum(jnp.where(hit, gate_values(codes)[:, :, None], 0.0), axis=1)


def widen(row_block, w_gate, w_up):
    return (
        jnp.dot(row_block, w_gate, preferred_element_type=jnp.float32),
        jnp.dot(row_block, w_up, preferred_element_type=jnp.float32),
    )


def dense_forward(parts, coef, w_down):
    gate_part, up_part = parts
    hidden = (gate_part * jax.nn.sigmoid(gate_part) * up_part * coef).astype(jnp.bfloat16)
    return jnp.dot(hidden, w_down, preferred_element_type=jnp.float32).astype(jnp.bfloat16)


def dense_backward(parts, grad_block, coef, w_gate, w_up, w_down):
    gate_part, up_part = parts
    sigmoid_part = jax.nn.sigmoid(gate_part)
    activated = gate_part * sigmoid_part
    slope = sigmoid_part * (1.0 + gate_part * (1.0 - sigmoid_part))
    hidden_grad = transposed(grad_block, w_down) * coef
    gate_grad = (hidden_grad * up_part * slope).astype(jnp.bfloat16)
    up_grad = (hidden_grad * activated).astype(jnp.bfloat16)
    return (transposed(gate_grad, w_gate) + transposed(up_grad, w_up)).astype(jnp.bfloat16)


UP, DOWN, SIDE, PAIR = range(4)
PARTS = 4
RELAYED = tuple((p, 0) for p in range(1, PARTS)) + ((0, 0), (0, 1))
ENDING = tuple((p, 1) for p in range(1, PARTS))


def position(n_peer):
    me = lax.axis_index("expert")
    return me, me // 4, me // 2 % 2, me % 2, n_peer // 4


def block_at(z, y, c):
    return (z * 2 + y) * 2 + c


def greet_neighbours(z, y, c, n_z, extra=()):
    barrier = pltpu.get_barrier_semaphore()

    def greet(peer):
        pl.semaphore_signal(barrier, inc=1, device_id={"expert": peer})

    greet(block_at(z, 1 - y, c))
    greet(block_at(z, y, 1 - c))

    @pl.when(z < n_z - 1)
    def _():
        greet(block_at(z + 1, y, c))

    @pl.when(z > 0)
    def _():
        greet(block_at(z - 1, y, c))

    pl.semaphore_wait(barrier, 2 + jnp.minimum(z, 1) + jnp.minimum(n_z - 1 - z, 1))


def greet_all(me, n_peer):
    barrier = pltpu.get_barrier_semaphore()

    def greet(step, carry):
        pl.semaphore_signal(barrier, inc=1, device_id={"expert": lax.rem(me + step, n_peer)})
        return carry

    lax.fori_loop(1, n_peer, greet, 0)
    pl.semaphore_wait(barrier, n_peer - 1)


def gather_kernel(n_rows, with_coef, n_peer, *refs):
    count = n_rows + with_coef
    ins, outs, sems = refs[:count], refs[count : 2 * count], refs[2 * count :]
    send_sem, recv_sem, own_sem = sems[:3]
    me, z, y, c, n_z = position(n_peer)
    half = ins[0].shape[0] // PARTS
    target = (
        block_at(z + 1, y, c),
        block_at(z - 1, y, c),
        block_at(z, 1 - y, c),
        block_at(z, y, 1 - c),
    )
    if with_coef:
        greet_all(me, n_peer)
    else:
        greet_neighbours(z, y, c, n_z)
    own_copies = [
        pltpu.make_async_copy(ins[r], outs[r].at[me], own_sem.at[r]) for r in range(n_rows)
    ]
    for own in own_copies:
        own.start()

    def coef_copy(step):
        peer = lax.rem(me + step, n_peer)
        return pltpu.make_async_remote_copy(
            src_ref=ins[n_rows].at[peer],
            dst_ref=outs[n_rows].at[me],
            send_sem=sems[3].at[step],
            recv_sem=sems[4].at[step],
            device_id={"expert": peer},
        )

    def piece_copy(r, way, block, part, own):
        rows = pl.ds(part * half, half)
        return pltpu.make_async_remote_copy(
            src_ref=ins[r].at[rows] if own else outs[r].at[block, rows],
            dst_ref=outs[r].at[block, rows],
            send_sem=send_sem.at[r, way, block, part],
            recv_sem=recv_sem.at[r, block, part],
            device_id={"expert": target[way]},
        )

    def ways_of(offset, other, part):
        if part > 0 and other:
            return (PAIR,)
        along = (UP, DOWN) if offset == 0 else (UP,) if offset < 0 else (DOWN,)
        aside = (SIDE,) if not other and (part > 0 or offset == 0) else ()
        return along + aside + (PAIR,)

    def each_way(offset, other, part, act):
        for way in ways_of(offset, other, part):
            if way == UP:
                pl.when(z < n_z - 1)(functools.partial(act, way))
            elif way == DOWN:
                pl.when(z > 0)(functools.partial(act, way))
            else:
                act(way)

    def each_piece(act):
        for pieces in (RELAYED, ENDING):
            for distance in range(n_z):
                for offset in (0,) if distance == 0 else (-distance, distance):

                    @pl.when((z + offset >= 0) & (z + offset < n_z))
                    def _():
                        for part, other in pieces:
                            for r in range(n_rows):
                                act(r, offset, other, part)

    def send(r, offset, other, part):
        block = block_at(z + offset, 1 - y if other else y, c)
        own = offset == 0 and not other
        if not own:
            piece_copy(r, PAIR, block, part, False).wait_recv()
        each_way(
            offset, other, part, lambda way: piece_copy(r, way, block, part, own).start()
        )

    def drain(r, offset, other, part):
        block = block_at(z + offset, 1 - y if other else y, c)
        own = offset == 0 and not other
        each_way(
            offset, other, part, lambda way: piece_copy(r, way, block, part, own).wait_send()
        )

    if with_coef:
        own_coef = pltpu.make_async_copy(
            ins[n_rows].at[me], outs[n_rows].at[me], own_sem.at[n_rows]
        )
        own_coef.start()
        for step in range(1, n_peer):
            coef_copy(step).start()
    each_piece(send)
    for r in range(n_rows):
        for spot in range(2 * n_z):
            for part in range(PARTS):
                piece_copy(r, PAIR, spot * 2 + 1 - c, part, False).wait_recv()
    each_piece(drain)
    for own in own_copies:
        own.wait()
    if with_coef:
        own_coef.wait()
        for step in range(1, n_peer):
            coef_copy(step).wait_recv()
            coef_copy(step).wait_send()


def relay_gather(rows, coef, ident):
    n_peer = lax.axis_size("expert")
    n_rows, with_coef = len(rows), int(coef is not None)
    shapes = [jax.ShapeDtypeStruct((n_peer,) + r.shape, r.dtype) for r in rows]
    scratch = [
        pltpu.SemaphoreType.DMA((n_rows, 4, n_peer, PARTS)),
        pltpu.SemaphoreType.DMA((n_rows, n_peer, PARTS)),
        pltpu.SemaphoreType.DMA((n_rows + 1,)),
    ]
    operands = list(rows)
    if with_coef:
        operands.append(coef)
        shapes.append(jax.ShapeDtypeStruct(coef.shape, coef.dtype))
        scratch += [pltpu.SemaphoreType.DMA((n_peer,))] * 2
    return pl.pallas_call(
        functools.partial(gather_kernel, n_rows, with_coef, n_peer),
        out_shape=shapes,
        in_specs=[pl.BlockSpec(memory_space=pltpu.VMEM)] * len(operands),
        out_specs=[pl.BlockSpec(memory_space=pltpu.VMEM)] * len(operands),
        scratch_shapes=scratch,
        compiler_params=pltpu.CompilerParams(collective_id=ident, has_side_effects=True),
        name="relay_gather_%d" % ident,
    )(*operands)


def scatter_kernel(n_peer, in_ref, out_ref, acc, paired, chained, sided, last, *sems):
    pair_send, pair_recv, chain_send, chain_recv, side_send, side_recv = sems
    me, z, y, c, n_z = position(n_peer)
    sizes = (out_ref.shape[0] // 2, out_ref.shape[0] - out_ref.shape[0] // 2)
    greet_neighbours(z, y, c, n_z)

    def rows_of(part):
        return pl.ds(part * sizes[0], sizes[part])

    def pair_copy(zb, yb):
        return pltpu.make_async_remote_copy(
            src_ref=in_ref.at[block_at(zb, yb, 1 - c)],
            dst_ref=paired.at[zb, yb],
            send_sem=pair_send.at[zb, yb],
            recv_sem=pair_recv.at[zb, yb],
            device_id={"expert": block_at(z, y, 1 - c)},
        )

    def side_copy(zb):
        final = zb is None
        return pltpu.make_async_remote_copy(
            src_ref=acc.at[z, 1 - y, rows_of(1)] if final else acc.at[zb, 1 - y, rows_of(0)],
            dst_ref=last if final else sided.at[zb],
            send_sem=side_send.at[n_z if final else zb],
            recv_sem=side_recv.at[n_z if final else zb],
            device_id={"expert": block_at(z, 1 - y, c)},
        )

    kinds = ((1, 0), (1, 1), (0, 0))

    def chain_copy(way, zb, kind):
        part, other = kinds[kind]
        return pltpu.make_async_remote_copy(
            src_ref=acc.at[zb, 1 - y if other else y, rows_of(part)],
            dst_ref=chained.at[way, zb, kind, pl.ds(0, sizes[part])],
            send_sem=chain_send.at[way, zb, kind],
            recv_sem=chain_recv.at[way, zb, kind],
            device_id={"expert": block_at(z + (1, -1)[way], y, c)},
        )

    def add_to(zb, yb, part, other_ref):
        rows = rows_of(part)
        acc[zb, yb, rows] = (
            acc[zb, yb, rows].astype(jnp.float32) + other_ref[...].astype(jnp.float32)
        ).astype(acc.dtype)

    def chip_sum(zb, yb):
        pair_copy(zb, yb).wait_recv()
        mine = in_ref[block_at(zb, yb, c)].astype(jnp.float32)
        acc[zb, yb] = (mine + paired[zb, yb].astype(jnp.float32)).astype(acc.dtype)

    def has_source(way):
        return (z > 0) if way == 0 else (z < n_z - 1)

    def take_chain(way, zb, kind):
        part, other = kinds[kind]

        @pl.when(has_source(way))
        def _():
            chain_copy(way, zb, kind).wait_recv()
            add_to(zb, 1 - y if other else y, part, chained.at[way, zb, kind, pl.ds(0, sizes[part])])

    def each_chain(act):
        for distance in range(n_z - 1, 0, -1):
            for way, sign in ((0, 1), (1, -1)):
                zb = z + sign * distance
                pl.when((zb >= 0) & (zb < n_z))(functools.partial(act, way, zb))

    def take_side(zb):
        side_copy(zb).wait_recv()
        add_to(zb, y, 0, sided.at[zb])

    def start_pair(way, zb):
        pair_copy(zb, 1 - y).start()
        pair_copy(zb, y).start()

    def sum_pair(way, zb):
        chip_sum(zb, 1 - y)
        side_copy(zb).start()
        chip_sum(zb, y)

    def begin_chain(way, zb):
        sum_pair(way, zb)

        @pl.when(jnp.logical_not(has_source(way)))
        def _():
            for kind in range(2):
                chain_copy(way, zb, kind).start()

    def send_chain(way, zb):
        @pl.when(has_source(way))
        def _():
            for kind in range(2):
                take_chain(way, zb, kind)
                chain_copy(way, zb, kind).start()

        take_side(zb)
        take_chain(way, zb, 2)
        chain_copy(way, zb, 2).start()

    def drain_chain(way, zb):
        for kind in range(3):
            chain_copy(way, zb, kind).wait_send()

    each_chain(start_pair)
    start_pair(0, z)
    each_chain(begin_chain)
    sum_pair(0, z)
    each_chain(send_chain)
    for kind in (1, 0, 2):
        if kind == 2:
            take_side(z)
        for way in range(2):
            take_chain(way, z, kind)
        if kind == 1:
            side_copy(None).start()
    out_ref[rows_of(0)] = acc[z, y, rows_of(0)].astype(jnp.float32)
    side_copy(None).wait_recv()
    out_ref[rows_of(1)] = acc[z, y, rows_of(1)].astype(jnp.float32) + last[...].astype(
        jnp.float32
    )
    for yb in range(2):
        for zb in range(n_z):
            pair_copy(zb, yb).wait_send()
    for zb in list(range(n_z)) + [None]:
        side_copy(zb).wait_send()
    each_chain(drain_chain)


def relay_scatter(partial, ident):
    n_peer = lax.axis_size("expert")
    n_z = n_peer // 4
    width = partial.shape[-1]
    tokens = partial.shape[0] // n_peer
    first = tokens // 2
    kind = partial.dtype
    return pl.pallas_call(
        functools.partial(scatter_kernel, n_peer),
        out_shape=jax.ShapeDtypeStruct((tokens, width), jnp.float32),
        in_specs=[pl.BlockSpec(memory_space=pltpu.VMEM)],
        out_specs=pl.BlockSpec(memory_space=pltpu.VMEM),
        scratch_shapes=[
            pltpu.VMEM((n_z, 2, tokens, width), kind),
            pltpu.VMEM((n_z, 2, tokens, width), kind),
            pltpu.VMEM((2, n_z, 3, tokens - first, width), kind),
            pltpu.VMEM((n_z, first, width), kind),
            pltpu.VMEM((tokens - first, width), kind),
            pltpu.SemaphoreType.DMA((n_z, 2)),
            pltpu.SemaphoreType.DMA((n_z, 2)),
            pltpu.SemaphoreType.DMA((2, n_z, 3)),
            pltpu.SemaphoreType.DMA((2, n_z, 3)),
            pltpu.SemaphoreType.DMA((n_z + 1,)),
            pltpu.SemaphoreType.DMA((n_z + 1,)),
        ],
        compiler_params=pltpu.CompilerParams(collective_id=ident, has_side_effects=True),
        name="relay_scatter_%d" % ident,
    )(partial.reshape(n_peer, tokens, width))


def dense_body(boundary, saved, norm_gain, gate_weight, up_weight, down_weight, routes, gate_codes):
    first = lax.axis_index("segment") == 0
    n_peer = lax.axis_size("expert")
    weights = (gate_weight[0, 0], up_weight[0, 0], down_weight[0, 0])
    gain_row = norm_gain[0]
    edge_rows = boundary[0]
    stored = saved[0]
    inputs_now = jnp.where(first, edge_rows, stored)
    widened, scaling, normed = normalize(inputs_now, gain_row)
    early_rows = jnp.where(first, normalize(stored, gain_row)[2], edge_rows)
    coef_f = coefficients(routes[0, 0], gate_codes[0, 0], n_peer)
    coef_b = coefficients(routes[0, 1], gate_codes[0, 1], n_peer)
    coef = jnp.stack([coef_f.T, coef_b.T], axis=1)
    rows_now, rows_early, coef_all = relay_gather((normed, early_rows), coef, 1)
    flat = (-1, normed.shape[-1])
    rows_early = rows_early.reshape(flat)
    coef_f = coef_all[:, 0].reshape(-1, 1)
    coef_b = coef_all[:, 1].reshape(-1, 1)
    w_gate, w_up, w_down = weights
    parts = widen(rows_now.reshape(flat), w_gate, w_up)
    partial, parts_kept = lax.cond(
        first,
        lambda: (dense_forward(parts, coef_f, w_down), widen(rows_early, w_gate, w_up)),
        lambda: (dense_backward(parts, rows_early, coef_b, *weights), parts),
    )
    produced = finish(widened, scaling, gain_row, edge_rows, relay_scatter(partial, 2), first)
    n_segment = lax.axis_size("segment")
    arrived = lax.ppermute(produced, "segment", [(i, n_segment - 1 - i) for i in range(n_segment)])
    inputs_next = jnp.where(first, stored, arrived)
    widened_next, scaling_next, normed_next = normalize(inputs_next, gain_row)
    landed = relay_gather((jnp.where(first, arrived, normed_next),), None, 3)[0].reshape(flat)
    partial = lax.cond(
        first,
        lambda: dense_backward(parts_kept, landed, coef_b, *weights),
        lambda: dense_forward(widen(landed, w_gate, w_up), coef_f, w_down),
    )
    result = finish(
        widened_next, scaling_next, gain_row, arrived, relay_scatter(partial, 4), jnp.logical_not(first)
    )
    return result[None]


def body(*arrays):
    tokens, top_count = arrays[0].shape[1], arrays[6].shape[3]
    n_peer = lax.axis_size("expert")
    capacity = max(2, 3 * tokens * top_count // (2 * n_peer))
    chosen = dense_body if tokens <= 2 * capacity and n_peer % 4 == 0 else routed_body
    return chosen(*arrays)


def solution(mesh):
    return jax.shard_map(
        body,
        mesh=mesh,
        in_specs=(
            P("segment", "expert", None),
            P("segment", "expert", None),
            P("segment", None),
            P("segment", "expert", None, None),
            P("segment", "expert", None, None),
            P("segment", "expert", None, None),
            P("segment", None, "expert", None),
            P("segment", None, "expert", None),
        ),
        out_specs=P("segment", "expert", None),
        check_vma=False,
    )
```

```python
import functools

import jax
import jax.numpy as jnp
from jax import lax
from jax.experimental import pallas as pl
from jax.experimental.pallas import tpu as pltpu
from jax.sharding import PartitionSpec as P

epsilon = 1e-06


def shifted(block, axis, distance):
    devices = range(lax.axis_size(axis))
    route = [(i - distance, i) for i in devices if i - distance in devices]
    return lax.ppermute(block, axis, route)


def gate_values(codes):
    counted = codes.astype(jnp.float32)
    return counted / jnp.sum(counted, axis=-1, keepdims=True)


def normalize(inputs, gain_row):
    widened = inputs.astype(jnp.float32)
    scaling = lax.rsqrt(jnp.mean(widened * widened, axis=-1, keepdims=True) + epsilon)
    return (widened, scaling, (widened * scaling * gain_row).astype(jnp.bfloat16))


def transposed(left, right):
    return lax.dot_general(
        left, right, (((1,), (1,)), ((), ())), preferred_element_type=jnp.float32
    )


def expert_forward(row_block, w_gate, w_up, w_down):
    gate_part = jnp.dot(row_block, w_gate, preferred_element_type=jnp.float32)
    up_part = jnp.dot(row_block, w_up, preferred_element_type=jnp.float32)
    hidden = (gate_part * jax.nn.sigmoid(gate_part) * up_part).astype(jnp.bfloat16)
    return jnp.dot(hidden, w_down, preferred_element_type=jnp.float32).astype(jnp.bfloat16)


def expert_backward(row_block, grad_block, w_gate, w_up, w_down):
    gate_part = jnp.dot(row_block, w_gate, preferred_element_type=jnp.float32)
    up_part = jnp.dot(row_block, w_up, preferred_element_type=jnp.float32)
    sigmoid_part = jax.nn.sigmoid(gate_part)
    activated = gate_part * sigmoid_part
    slope = sigmoid_part * (1.0 + gate_part * (1.0 - sigmoid_part))
    hidden_grad = transposed(grad_block, w_down)
    gate_grad = (hidden_grad * up_part * slope).astype(jnp.bfloat16)
    up_grad = (hidden_grad * activated).astype(jnp.bfloat16)
    return (transposed(gate_grad, w_gate) + transposed(up_grad, w_up)).astype(jnp.bfloat16)


def layout(route, codes, n_peer, capacity):
    tokens, top_count = route.shape
    flat_ids = route.reshape(-1)
    onehot = (flat_ids[:, None] == jnp.arange(n_peer, dtype=jnp.int32)[None, :]).astype(jnp.int32)
    spots = jnp.arange(flat_ids.shape[0], dtype=jnp.int32)
    earlier = (spots[None, :] < spots[:, None]).astype(jnp.bfloat16)
    before = jnp.dot(earlier, onehot.astype(jnp.bfloat16), preferred_element_type=jnp.float32)
    rank_in = jnp.sum(before.astype(jnp.int32) * onehot, axis=1)
    slot_of = flat_ids * capacity + rank_in
    slot_ids = jnp.arange(n_peer * capacity, dtype=jnp.int32)
    slot_hit = (slot_ids[:, None, None] == slot_of.reshape(tokens, top_count)[None, :, :]).astype(
        jnp.bfloat16
    )
    placing = jnp.sum(slot_hit, axis=2, dtype=jnp.float32).astype(jnp.bfloat16)
    return (placing, slot_of, gate_values(codes))


def dispatch(placing, payload, n_peer, capacity):
    picked = jnp.dot(placing, payload, preferred_element_type=jnp.float32).astype(jnp.bfloat16)
    return picked.reshape(n_peer, capacity, payload.shape[-1])


def collect(slot_of, gates, came_back):
    flat_rows = came_back.reshape(-1, came_back.shape[-1])
    chosen = jnp.take(flat_rows, slot_of, axis=0).reshape(
        gates.shape[0], gates.shape[1], flat_rows.shape[-1]
    )
    return jnp.einsum("tk,tkd->td", gates, chosen.astype(jnp.float32))


def apply_expert(forward_flag, first_rows, second_rows, weights):
    layout_of = first_rows.shape
    row_block = first_rows.reshape(-1, layout_of[-1])
    grad_block = second_rows.reshape(-1, layout_of[-1])
    outcome = lax.cond(
        forward_flag,
        lambda: expert_forward(row_block, weights[0], weights[1], weights[2]),
        lambda: expert_backward(row_block, grad_block, weights[0], weights[1], weights[2]),
    )
    return outcome.reshape(layout_of)


def return_rows(outcome):
    return lax.all_to_all(outcome, "expert", split_axis=0, concat_axis=0, tiled=True)


def finish(widened, scaling, gain_row, upstream, summed, forward_flag):
    forward_out = widened + summed
    scaled = summed * gain_row
    inner_mean = jnp.mean(scaled * widened, axis=-1, keepdims=True)
    cubed = scaling * scaling * scaling
    backward_out = upstream.astype(jnp.float32) + scaling * scaled - widened * cubed * inner_mean
    return jnp.where(forward_flag, forward_out, backward_out).astype(jnp.bfloat16)


def routed_body(boundary, saved, norm_gain, gate_weight, up_weight, down_weight, routes, gate_codes):
    first_segment = lax.axis_index("segment") == 0
    later_forward = jnp.logical_not(first_segment)
    n_peer = lax.axis_size("expert")
    tokens = boundary.shape[1]
    top_count = routes.shape[3]
    capacity = max(2, 3 * tokens * top_count // (2 * n_peer))
    weights = (gate_weight[0, 0], up_weight[0, 0], down_weight[0, 0])
    gain_row = norm_gain[0]
    edge_rows = boundary[0]
    stored = saved[0]
    route_now = jnp.where(first_segment, routes[0, 0], routes[0, 1])
    codes_now = jnp.where(first_segment, gate_codes[0, 0], gate_codes[0, 1])
    route_next = jnp.where(first_segment, routes[0, 1], routes[0, 0])
    codes_next = jnp.where(first_segment, gate_codes[0, 1], gate_codes[0, 0])
    place_now, slots_now, gates_now = layout(route_now, codes_now, n_peer, capacity)
    place_next, slots_next, gates_next = layout(route_next, codes_next, n_peer, capacity)
    inputs_now = jnp.where(first_segment, edge_rows, stored)
    widened, scaling, normed = normalize(inputs_now, gain_row)
    stored_normed = normalize(stored, gain_row)[2]
    early_rows = jnp.where(first_segment, stored_normed, edge_rows)
    early_place = jnp.where(first_segment, place_next, place_now)
    outgoing = (
        dispatch(place_now, normed, n_peer, capacity),
        dispatch(early_place, early_rows, n_peer, capacity),
    )
    paired = (
        lax.all_to_all(outgoing[0], "expert", split_axis=0, concat_axis=0, tiled=True),
        lax.all_to_all(outgoing[1], "expert", split_axis=0, concat_axis=0, tiled=True),
    )
    outcome = apply_expert(first_segment, paired[0], paired[1], weights)
    came_back = return_rows(outcome)
    kept_rows = paired[1]
    produced = finish(
        widened,
        scaling,
        gain_row,
        edge_rows,
        collect(slots_now, gates_now, came_back),
        first_segment,
    )
    arrived = shifted(produced, "segment", 1) + shifted(produced, "segment", -1)
    inputs_next = jnp.where(first_segment, stored, arrived)
    widened_next, scaling_next, normed_next = normalize(inputs_next, gain_row)
    member = jnp.where(first_segment, arrived, normed_next)
    landed = lax.all_to_all(
        dispatch(place_next, member, n_peer, capacity),
        "expert",
        split_axis=0,
        concat_axis=0,
        tiled=True,
    )
    outcome = apply_expert(
        later_forward, jnp.where(first_segment, kept_rows, landed), landed, weights
    )
    came_next = return_rows(outcome)
    result = finish(
        widened_next,
        scaling_next,
        gain_row,
        arrived,
        collect(slots_next, gates_next, came_next),
        later_forward,
    )
    return result[None]


PIECES = 2
INFO = 128
STRIP = 256
MESH = pl.DeviceIdType.MESH


def position(n_peer):
    me = lax.axis_index("expert")
    return me, me // 4, me // 2 % 2, me % 2, n_peer // 4


def block_at(z, y, c):
    return (z * 2 + y) * 2 + c


def nearest_first(z, n_z):
    tables = []
    for at in range(n_z):
        inward = 1 if 2 * at < n_z else -1
        steps = [0] + [s * d for d in range(1, n_z) for s in (inward, -inward)]
        tables.append([at + s for s in steps if 0 <= at + s < n_z])
    order = []
    for i in range(n_z):
        chosen = jnp.int32(tables[0][i])
        for at in range(1, n_z):
            chosen = jnp.where(z == at, jnp.int32(tables[at][i]), chosen)
        order.append(chosen)
    return order


def rms_scale(rows):
    return lax.rsqrt(jnp.mean(rows * rows, axis=-1, keepdims=True) + epsilon)


def section_kernel(n_peer, top_count, *refs):
    edge_ref, stored_ref, gain_ref, info_ref, wg_in, wu_in, wd_in, out_ref = refs[:8]
    s_rows, e_rows, wg, wu, wd, kept_g, kept_u, mid_a, mid_b = refs[8:17]
    partial, paired, acc, crossed, chained, base_next, produced = refs[17:24]
    w_sem, z_send, z_recv, y_send, y_recv, p_send, p_recv = refs[24:31]
    q_send, q_recv, s_send, s_recv, c_send, c_recv, x_send, x_recv = refs[31:]
    first = lax.axis_index("segment") == 0
    other_segment = 1 - lax.axis_index("segment")
    me, z, y, c, n_z = position(n_peer)
    tokens, width = edge_ref.shape
    hidden = wg.shape[1]
    plane_rows = 4 * tokens
    piece = tokens // PIECES
    order = nearest_first(z, n_z)

    def rows_of(p):
        return pl.ds(p * piece, piece)

    def ok(plane):
        return (plane >= 0) & (plane < n_z)

    loads = [
        pltpu.make_async_copy(src, dst, w_sem.at[i])
        for i, (src, dst) in enumerate(((wg_in, wg), (wu_in, wu), (wd_in, wd)))
    ]
    for load in loads:
        load.start()

    barrier = pltpu.get_barrier_semaphore()

    def greet(**peer):
        pl.semaphore_signal(barrier, inc=1, device_id=peer, device_id_type=MESH)

    greet(expert=block_at(z, 1 - y, c))
    greet(expert=block_at(z, y, 1 - c))
    greet(segment=other_segment)
    pl.when(z < n_z - 1)(lambda: greet(expert=block_at(z + 1, y, c)))
    pl.when(z > 0)(lambda: greet(expert=block_at(z - 1, y, c)))

    def block(stage, index, p):
        if stage == 0:
            return s_rows.at[index, rows_of(p)]
        return e_rows.at[stage - 1, index, rows_of(p)]

    def remote(ref, send, recv, **peer):
        return pltpu.make_async_remote_copy(
            src_ref=ref, dst_ref=ref, send_sem=send, recv_sem=recv, device_id=peer, device_id_type=MESH
        )

    def z_copy(stage, plane, way, p):
        return remote(
            block(stage, block_at(plane, y, c), p),
            z_send.at[stage, plane, way, p],
            z_recv.at[stage, plane, p],
            expert=block_at(z + 1 - 2 * way, y, c),
        )

    def y_copy(stage, plane, p, column):
        return remote(
            block(stage, block_at(plane, column, c), p),
            y_send.at[stage, plane, p],
            y_recv.at[stage, plane, p],
            expert=block_at(z, 1 - y, c),
        )

    def p_copy(stage, plane, column, p, core):
        return remote(
            block(stage, block_at(plane, column, core), p),
            p_send.at[stage, plane, column, p],
            p_recv.at[stage, plane, column, p],
            expert=block_at(z, y, 1 - c),
        )

    def send_own(stage, p):
        y_copy(stage, z, p, y).start()
        pl.when(z < n_z - 1)(lambda: z_copy(stage, z, 0, p).start())
        pl.when(z > 0)(lambda: z_copy(stage, z, 1, p).start())
        p_copy(stage, z, y, p, c).start()

    def arrivals(stage, distance):
        for p in range(PIECES):
            for d in (distance, -distance):
                plane, way, onward = z + d, int(d > 0), z - d // distance

                @pl.when(ok(plane))
                def _():
                    z_copy(stage, plane, way, p).wait_recv()
                    pl.when(ok(onward))(lambda: z_copy(stage, plane, way, p).start())
                    y_copy(stage, plane, p, y).start()
                    p_copy(stage, plane, y, p, c).start()

    def plane_ready(stage, plane):
        for p in range(PIECES):
            y_copy(stage, plane, p, 1 - y).wait_recv()
            p_copy(stage, plane, 1 - y, p, c).start()
        for column in range(2):
            for p in range(PIECES):
                p_copy(stage, plane, column, p, 1 - c).wait_recv()

    def drain_gather(stage):
        for p in range(PIECES):
            for i in range(n_z):
                y_copy(stage, i, p, y).wait_send()
                for column in range(2):
                    p_copy(stage, i, column, p, c).wait_send()
            pl.when(z < n_z - 1)(lambda: z_copy(stage, z, 0, p).wait_send())
            pl.when(z > 0)(lambda: z_copy(stage, z, 1, p).wait_send())
            for distance in range(1, n_z):
                for d in (distance, -distance):
                    plane, way, onward = z + d, int(d > 0), z - d // distance
                    pl.when(ok(plane) & ok(onward))(
                        lambda: z_copy(stage, plane, way, p).wait_send()
                    )

    def plane_of(plane):
        return pl.ds(plane * 4, 4)

    def gates_of(plane, offset):
        info = s_rows[plane_of(plane), :, width : width + INFO].reshape(plane_rows, INFO)
        info = info.astype(jnp.float32)
        route = info[:, offset : offset + top_count]
        codes = info[:, offset + top_count : offset + 2 * top_count]
        mine = jnp.where(route == me.astype(jnp.float32), codes, 0.0)
        return jnp.sum(mine, axis=-1, keepdims=True) / jnp.sum(codes, axis=-1, keepdims=True)

    strips = [pl.ds(i, STRIP) for i in range(0, hidden, STRIP)]
    wide = [pl.ds(i, 2 * STRIP) for i in range(0, width, 2 * STRIP)]

    def widen(plane):
        rows = s_rows[plane_of(plane), :, 0:width].reshape(plane_rows, width)
        for strip in strips:
            kept_g[plane, :, strip] = jnp.dot(
                rows, wg[:, strip], preferred_element_type=jnp.float32
            )
            kept_u[plane, :, strip] = jnp.dot(
                rows, wu[:, strip], preferred_element_type=jnp.float32
            )

    def keep(plane, columns, value):
        partial[plane_of(plane), :, columns] = value.astype(jnp.bfloat16).reshape(
            4, tokens, value.shape[-1]
        )

    def forward(phase, plane):
        rows = e_rows[phase, plane_of(plane)].reshape(plane_rows, width)
        coef = gates_of(plane, 0)
        for strip in strips:
            gate_part = jnp.dot(rows, wg[:, strip], preferred_element_type=jnp.float32)
            up_part = jnp.dot(rows, wu[:, strip], preferred_element_type=jnp.float32)
            mid_a[:, strip] = (gate_part * jax.nn.sigmoid(gate_part) * up_part * coef).astype(
                jnp.bfloat16
            )
        for columns in wide:
            keep(
                plane,
                columns,
                jnp.dot(mid_a[...], wd[:, columns], preferred_element_type=jnp.float32),
            )

    def backward(phase, plane):
        rows = e_rows[phase, plane_of(plane)].reshape(plane_rows, width)
        coef = gates_of(plane, 2 * top_count)
        for strip in strips:
            hidden_grad = transposed(rows, wd[strip, :]) * coef
            gate_part, up_part = kept_g[plane, :, strip], kept_u[plane, :, strip]
            sigmoid_part = jax.nn.sigmoid(gate_part)
            slope = sigmoid_part * (1.0 + gate_part * (1.0 - sigmoid_part))
            mid_a[:, strip] = (hidden_grad * up_part * slope).astype(jnp.bfloat16)
            mid_b[:, strip] = (hidden_grad * gate_part * sigmoid_part).astype(jnp.bfloat16)
        for columns in wide:
            keep(
                plane,
                columns,
                transposed(mid_a[...], wg[columns, :]) + transposed(mid_b[...], wu[columns, :]),
            )

    def q_copy(plane, column):
        return pltpu.make_async_remote_copy(
            src_ref=partial.at[block_at(plane, column, 1 - c)],
            dst_ref=paired.at[plane, column],
            send_sem=q_send.at[plane, column],
            recv_sem=q_recv.at[plane, column],
            device_id={"expert": block_at(z, y, 1 - c)},
            device_id_type=MESH,
        )

    def s_copy(plane, p):
        return pltpu.make_async_remote_copy(
            src_ref=acc.at[plane, 1 - y, rows_of(p)],
            dst_ref=crossed.at[plane, rows_of(p)],
            send_sem=s_send.at[plane, p],
            recv_sem=s_recv.at[plane, p],
            device_id={"expert": block_at(z, 1 - y, c)},
            device_id_type=MESH,
        )

    def c_copy(way, plane, p):
        return pltpu.make_async_remote_copy(
            src_ref=acc.at[plane, y, rows_of(p)],
            dst_ref=chained.at[way, plane, rows_of(p)],
            send_sem=c_send.at[plane, p],
            recv_sem=c_recv.at[way, plane, p],
            device_id={"expert": block_at(z + 1 - 2 * way, y, c)},
            device_id_type=MESH,
        )

    def start_pair(plane):
        for column in range(2):
            q_copy(plane, column).start()

    def chip_sum(plane):
        for column in (1 - y, y):
            q_copy(plane, column).wait_recv()
            mine = partial[block_at(plane, column, c)].astype(jnp.float32)
            acc[plane, column] = (mine + paired[plane, column].astype(jnp.float32)).astype(acc.dtype)

    def start_side(plane):
        for p in range(PIECES):
            s_copy(plane, p).start()

    def take_side(plane, p):
        s_copy(plane, p).wait_recv()
        rows = rows_of(p)
        return acc[plane, y, rows].astype(jnp.float32) + crossed[plane, rows].astype(jnp.float32)

    def pass_on(plane, between):
        way = (plane < z).astype(jnp.int32)
        has_source = jnp.where(plane > z, z, n_z - 1 - z) > 0
        for p in range(PIECES):
            rows = rows_of(p)
            acc[plane, y, rows] = take_side(plane, p).astype(acc.dtype)
            if p == 0:
                between()

            @pl.when(has_source)
            def _():
                c_copy(way, plane, p).wait_recv()
                acc[plane, y, rows] = (
                    acc[plane, y, rows].astype(jnp.float32)
                    + chained[way, plane, rows].astype(jnp.float32)
                ).astype(acc.dtype)

            c_copy(way, plane, p).start()

    def finish_piece(forward_flag, base, p):
        rows = rows_of(p)
        summed = take_side(z, p)
        for way, there in ((0, z > 0), (1, z < n_z - 1)):
            pl.when(there)(lambda: c_copy(way, z, p).wait_recv())
            summed = summed + jnp.where(there, chained[way, z, rows].astype(jnp.float32), 0.0)
        base_rows = base[rows].astype(jnp.float32)
        stored = stored_ref[rows].astype(jnp.float32)
        scaling = rms_scale(stored)
        scaled = summed * gain_ref[...]
        inner = jnp.mean(scaled * stored, axis=-1, keepdims=True)
        change = scaling * scaled - stored * (scaling * scaling * scaling * inner)
        return (base_rows + jnp.where(forward_flag, summed, change)).astype(jnp.bfloat16)

    def entering(forward_flag, rows):
        wide_rows = rows.astype(jnp.float32)
        normed = wide_rows * rms_scale(wide_rows) * gain_ref[...]
        return jnp.where(forward_flag, normed, wide_rows).astype(jnp.bfloat16)

    def x_copy(p):
        return pltpu.make_async_remote_copy(
            src_ref=produced.at[rows_of(p)],
            dst_ref=base_next.at[rows_of(p)],
            send_sem=x_send.at[p],
            recv_sem=x_recv.at[p],
            device_id={"segment": other_segment},
            device_id_type=MESH,
        )

    def run_phase(phase, forward_flag, finishing):
        stage = phase + 1

        def compute(plane):
            pl.when(forward_flag)(lambda: forward(phase, plane))
            pl.when(jnp.logical_not(forward_flag))(lambda: backward(phase, plane))
            start_pair(plane)

        for i in range(n_z):
            if i < n_z - 1:
                arrivals(stage, i + 1)
            plane_ready(stage, order[i])
            compute(order[i])
            if i == n_z - 2:
                chip_sum(order[i])
                start_side(order[i])
        chip_sum(order[n_z - 1])
        start_side(order[n_z - 1])
        for i in range(n_z - 2):
            chip_sum(order[i])
        for i in range(n_z - 1, 0, -1):

            def between():
                if i == n_z - 1:
                    start_side(order[n_z - 3])
                elif i <= n_z - 3:
                    start_side(order[i - 1])

            pass_on(order[i], between)
        for p in range(PIECES):
            finishing(p)
        for i in range(n_z):
            for column in range(2):
                q_copy(i, column).wait_send()
            for p in range(PIECES):
                s_copy(i, p).wait_send()
        for i in range(1, n_z):
            for p in range(PIECES):
                c_copy((order[i] < z).astype(jnp.int32), order[i], p).wait_send()

    own = block_at(z, y, c)
    s_rows[own, :, 0:width] = entering(True, stored_ref[...])
    s_rows[own, :, width : width + INFO] = info_ref[...]
    pl.semaphore_wait(barrier, 3 + jnp.minimum(z, 1) + jnp.minimum(n_z - 1 - z, 1))
    for p in range(PIECES):
        send_own(0, p)
    e_rows[0, own] = entering(first, edge_ref[...])
    for i in range(n_z):
        if i < n_z - 1:
            arrivals(0, i + 1)
        if i == n_z - 2:
            for p in range(PIECES):
                send_own(1, p)
        plane_ready(0, order[i])
        if i == 0:
            loads[0].wait()
            loads[1].wait()
        widen(order[i])
    loads[2].wait()

    def hand_over(p):
        produced[rows_of(p)] = finish_piece(first, edge_ref, p)
        x_copy(p).start()

    run_phase(0, first, hand_over)
    for p in range(PIECES):
        rows = rows_of(p)
        x_copy(p).wait_recv()
        e_rows[1, own, rows] = entering(jnp.logical_not(first), base_next[rows])
        send_own(2, p)

    def deliver(p):
        out_ref[rows_of(p)] = finish_piece(jnp.logical_not(first), base_next, p)

    run_phase(1, jnp.logical_not(first), deliver)
    for p in range(PIECES):
        x_copy(p).wait_send()
    for stage in range(3):
        drain_gather(stage)


def dense_body(boundary, saved, norm_gain, gate_weight, up_weight, down_weight, routes, gate_codes):
    n_peer = lax.axis_size("expert")
    n_z = n_peer // 4
    tokens, width = boundary.shape[1:]
    hidden = gate_weight.shape[-1]
    top_count = routes.shape[-1]
    info = jnp.concatenate(
        [routes[0, 0], gate_codes[0, 0], routes[0, 1], gate_codes[0, 1]], axis=-1
    ).astype(jnp.bfloat16)
    info = jnp.pad(info, ((0, 0), (0, INFO - 4 * top_count)))
    kind, total = jnp.bfloat16, jnp.float32
    dma = pltpu.SemaphoreType.DMA
    result = pl.pallas_call(
        functools.partial(section_kernel, n_peer, top_count),
        out_shape=jax.ShapeDtypeStruct((tokens, width), kind),
        in_specs=[pl.BlockSpec(memory_space=pltpu.VMEM)] * 4
        + [pl.BlockSpec(memory_space=pl.ANY)] * 3,
        out_specs=pl.BlockSpec(memory_space=pltpu.VMEM),
        scratch_shapes=[
            pltpu.VMEM((n_peer, tokens, width + INFO), kind),
            pltpu.VMEM((2, n_peer, tokens, width), kind),
            pltpu.VMEM((width, hidden), kind),
            pltpu.VMEM((width, hidden), kind),
            pltpu.VMEM((hidden, width), kind),
            pltpu.VMEM((n_z, 4 * tokens, hidden), total),
            pltpu.VMEM((n_z, 4 * tokens, hidden), total),
            pltpu.VMEM((4 * tokens, hidden), kind),
            pltpu.VMEM((4 * tokens, hidden), kind),
            pltpu.VMEM((n_peer, tokens, width), kind),
            pltpu.VMEM((n_z, 2, tokens, width), kind),
            pltpu.VMEM((n_z, 2, tokens, width), kind),
            pltpu.VMEM((n_z, tokens, width), kind),
            pltpu.VMEM((2, n_z, tokens, width), kind),
            pltpu.VMEM((tokens, width), kind),
            pltpu.VMEM((tokens, width), kind),
            dma((3,)),
            dma((3, n_z, 2, PIECES)),
            dma((3, n_z, PIECES)),
            dma((3, n_z, PIECES)),
            dma((3, n_z, PIECES)),
            dma((3, n_z, 2, PIECES)),
            dma((3, n_z, 2, PIECES)),
            dma((n_z, 2)),
            dma((n_z, 2)),
            dma((n_z, PIECES)),
            dma((n_z, PIECES)),
            dma((n_z, PIECES)),
            dma((2, n_z, PIECES)),
            dma((PIECES,)),
            dma((PIECES,)),
        ],
        compiler_params=pltpu.CompilerParams(
            collective_id=1, has_side_effects=True, vmem_limit_bytes=60 << 20
        ),
        cost_estimate=pl.CostEstimate(
            flops=2 * n_peer * tokens * width * hidden * 8,
            bytes_accessed=6 * width * hidden,
            transcendentals=0,
        ),
        name="two_sections",
    )(
        boundary[0],
        saved[0],
        norm_gain,
        info,
        gate_weight[0, 0],
        up_weight[0, 0],
        down_weight[0, 0],
    )
    return result[None]


def body(*arrays):
    tokens, top_count = arrays[0].shape[1], arrays[6].shape[3]
    n_peer = lax.axis_size("expert")
    capacity = max(2, 3 * tokens * top_count // (2 * n_peer))
    planes = n_peer % 4 == 0 and n_peer >= 12 and lax.axis_size("segment") == 2
    chosen = dense_body if tokens <= 2 * capacity and planes else routed_body
    return chosen(*arrays)


def solution(mesh):
    return jax.shard_map(
        body,
        mesh=mesh,
        in_specs=(
            P("segment", "expert", None),
            P("segment", "expert", None),
            P("segment", None),
            P("segment", "expert", None, None),
            P("segment", "expert", None, None),
            P("segment", "expert", None, None),
            P("segment", None, "expert", None),
            P("segment", None, "expert", None),
        ),
        out_specs=P("segment", "expert", None),
        check_vma=False,
    )
```

```python
import functools

import jax
import jax.numpy as jnp
from jax import lax
from jax.experimental import pallas as pl
from jax.experimental.pallas import tpu as pltpu
from jax.sharding import PartitionSpec as P

epsilon = 1e-06


def shifted(block, axis, distance):
    devices = range(lax.axis_size(axis))
    route = [(i - distance, i) for i in devices if i - distance in devices]
    return lax.ppermute(block, axis, route)


def gate_values(codes):
    counted = codes.astype(jnp.float32)
    return counted / jnp.sum(counted, axis=-1, keepdims=True)


def normalize(inputs, gain_row):
    widened = inputs.astype(jnp.float32)
    scaling = lax.rsqrt(jnp.mean(widened * widened, axis=-1, keepdims=True) + epsilon)
    return (widened, scaling, (widened * scaling * gain_row).astype(jnp.bfloat16))


def transposed(left, right):
    return lax.dot_general(
        left, right, (((1,), (1,)), ((), ())), preferred_element_type=jnp.float32
    )


def expert_forward(row_block, w_gate, w_up, w_down):
    gate_part = jnp.dot(row_block, w_gate, preferred_element_type=jnp.float32)
    up_part = jnp.dot(row_block, w_up, preferred_element_type=jnp.float32)
    hidden = (gate_part * jax.nn.sigmoid(gate_part) * up_part).astype(jnp.bfloat16)
    return jnp.dot(hidden, w_down, preferred_element_type=jnp.float32).astype(jnp.bfloat16)


def expert_backward(row_block, grad_block, w_gate, w_up, w_down):
    gate_part = jnp.dot(row_block, w_gate, preferred_element_type=jnp.float32)
    up_part = jnp.dot(row_block, w_up, preferred_element_type=jnp.float32)
    sigmoid_part = jax.nn.sigmoid(gate_part)
    activated = gate_part * sigmoid_part
    slope = sigmoid_part * (1.0 + gate_part * (1.0 - sigmoid_part))
    hidden_grad = transposed(grad_block, w_down)
    gate_grad = (hidden_grad * up_part * slope).astype(jnp.bfloat16)
    up_grad = (hidden_grad * activated).astype(jnp.bfloat16)
    return (transposed(gate_grad, w_gate) + transposed(up_grad, w_up)).astype(jnp.bfloat16)


def layout(route, codes, n_peer, capacity):
    tokens, top_count = route.shape
    flat_ids = route.reshape(-1)
    onehot = (flat_ids[:, None] == jnp.arange(n_peer, dtype=jnp.int32)[None, :]).astype(jnp.int32)
    spots = jnp.arange(flat_ids.shape[0], dtype=jnp.int32)
    earlier = (spots[None, :] < spots[:, None]).astype(jnp.bfloat16)
    before = jnp.dot(earlier, onehot.astype(jnp.bfloat16), preferred_element_type=jnp.float32)
    rank_in = jnp.sum(before.astype(jnp.int32) * onehot, axis=1)
    slot_of = flat_ids * capacity + rank_in
    slot_ids = jnp.arange(n_peer * capacity, dtype=jnp.int32)
    slot_hit = (slot_ids[:, None, None] == slot_of.reshape(tokens, top_count)[None, :, :]).astype(
        jnp.bfloat16
    )
    placing = jnp.sum(slot_hit, axis=2, dtype=jnp.float32).astype(jnp.bfloat16)
    return (placing, slot_of, gate_values(codes))


def dispatch(placing, payload, n_peer, capacity):
    picked = jnp.dot(placing, payload, preferred_element_type=jnp.float32).astype(jnp.bfloat16)
    return picked.reshape(n_peer, capacity, payload.shape[-1])


def collect(slot_of, gates, came_back):
    flat_rows = came_back.reshape(-1, came_back.shape[-1])
    chosen = jnp.take(flat_rows, slot_of, axis=0).reshape(
        gates.shape[0], gates.shape[1], flat_rows.shape[-1]
    )
    return jnp.einsum("tk,tkd->td", gates, chosen.astype(jnp.float32))


def apply_expert(forward_flag, first_rows, second_rows, weights):
    layout_of = first_rows.shape
    row_block = first_rows.reshape(-1, layout_of[-1])
    grad_block = second_rows.reshape(-1, layout_of[-1])
    outcome = lax.cond(
        forward_flag,
        lambda: expert_forward(row_block, weights[0], weights[1], weights[2]),
        lambda: expert_backward(row_block, grad_block, weights[0], weights[1], weights[2]),
    )
    return outcome.reshape(layout_of)


def return_rows(outcome):
    return lax.all_to_all(outcome, "expert", split_axis=0, concat_axis=0, tiled=True)


def finish(widened, scaling, gain_row, upstream, summed, forward_flag):
    forward_out = widened + summed
    scaled = summed * gain_row
    inner_mean = jnp.mean(scaled * widened, axis=-1, keepdims=True)
    cubed = scaling * scaling * scaling
    backward_out = upstream.astype(jnp.float32) + scaling * scaled - widened * cubed * inner_mean
    return jnp.where(forward_flag, forward_out, backward_out).astype(jnp.bfloat16)


def routed_body(boundary, saved, norm_gain, gate_weight, up_weight, down_weight, routes, gate_codes):
    first_segment = lax.axis_index("segment") == 0
    later_forward = jnp.logical_not(first_segment)
    n_peer = lax.axis_size("expert")
    tokens = boundary.shape[1]
    top_count = routes.shape[3]
    capacity = max(2, 3 * tokens * top_count // (2 * n_peer))
    weights = (gate_weight[0, 0], up_weight[0, 0], down_weight[0, 0])
    gain_row = norm_gain[0]
    edge_rows = boundary[0]
    stored = saved[0]
    route_now = jnp.where(first_segment, routes[0, 0], routes[0, 1])
    codes_now = jnp.where(first_segment, gate_codes[0, 0], gate_codes[0, 1])
    route_next = jnp.where(first_segment, routes[0, 1], routes[0, 0])
    codes_next = jnp.where(first_segment, gate_codes[0, 1], gate_codes[0, 0])
    place_now, slots_now, gates_now = layout(route_now, codes_now, n_peer, capacity)
    place_next, slots_next, gates_next = layout(route_next, codes_next, n_peer, capacity)
    inputs_now = jnp.where(first_segment, edge_rows, stored)
    widened, scaling, normed = normalize(inputs_now, gain_row)
    stored_normed = normalize(stored, gain_row)[2]
    early_rows = jnp.where(first_segment, stored_normed, edge_rows)
    early_place = jnp.where(first_segment, place_next, place_now)
    outgoing = (
        dispatch(place_now, normed, n_peer, capacity),
        dispatch(early_place, early_rows, n_peer, capacity),
    )
    paired = (
        lax.all_to_all(outgoing[0], "expert", split_axis=0, concat_axis=0, tiled=True),
        lax.all_to_all(outgoing[1], "expert", split_axis=0, concat_axis=0, tiled=True),
    )
    outcome = apply_expert(first_segment, paired[0], paired[1], weights)
    came_back = return_rows(outcome)
    kept_rows = paired[1]
    produced = finish(
        widened,
        scaling,
        gain_row,
        edge_rows,
        collect(slots_now, gates_now, came_back),
        first_segment,
    )
    arrived = shifted(produced, "segment", 1) + shifted(produced, "segment", -1)
    inputs_next = jnp.where(first_segment, stored, arrived)
    widened_next, scaling_next, normed_next = normalize(inputs_next, gain_row)
    member = jnp.where(first_segment, arrived, normed_next)
    landed = lax.all_to_all(
        dispatch(place_next, member, n_peer, capacity),
        "expert",
        split_axis=0,
        concat_axis=0,
        tiled=True,
    )
    outcome = apply_expert(
        later_forward, jnp.where(first_segment, kept_rows, landed), landed, weights
    )
    came_next = return_rows(outcome)
    result = finish(
        widened_next,
        scaling_next,
        gain_row,
        arrived,
        collect(slots_next, gates_next, came_next),
        later_forward,
    )
    return result[None]


PIECES = 2
INFO = 128
STRIP = 256
MESH = pl.DeviceIdType.MESH


def position(n_peer):
    me = lax.axis_index("expert")
    return me, me // 4, me // 2 % 2, me % 2, n_peer // 4


def block_at(z, y, c):
    return (z * 2 + y) * 2 + c


def nearest_first(z, n_z):
    tables = []
    for at in range(n_z):
        inward = 1 if 2 * at < n_z else -1
        steps = [0] + [s * d for d in range(1, n_z) for s in (inward, -inward)]
        tables.append([at + s for s in steps if 0 <= at + s < n_z])
    order = []
    for i in range(n_z):
        chosen = jnp.int32(tables[0][i])
        for at in range(1, n_z):
            chosen = jnp.where(z == at, jnp.int32(tables[at][i]), chosen)
        order.append(chosen)
    return order


def rms_scale(rows):
    return lax.rsqrt(jnp.mean(rows * rows, axis=-1, keepdims=True) + epsilon)


def section_kernel(n_peer, top_count, *refs):
    edge_ref, stored_ref, gain_ref, route_ref, code_ref, wg_in, wu_in, wd_in, out_ref = refs[:9]
    refs = refs[1:]
    s_rows, e_rows, wg, wu, wd, kept_g, kept_u, mid_a, mid_b = refs[8:17]
    partial, paired, acc, crossed, chained, base_next, produced = refs[17:24]
    w_sem, z_send, z_recv, y_send, y_recv, p_send, p_recv = refs[24:31]
    q_send, q_recv, s_send, s_recv, c_send, c_recv, x_send, x_recv = refs[31:]
    first = lax.axis_index("segment") == 0
    other_segment = 1 - lax.axis_index("segment")
    me, z, y, c, n_z = position(n_peer)
    tokens, width = edge_ref.shape
    hidden = wg.shape[1]
    plane_rows = 4 * tokens
    piece = tokens // PIECES
    order = nearest_first(z, n_z)

    def rows_of(p):
        return pl.ds(p * piece, piece)

    def ok(plane):
        return (plane >= 0) & (plane < n_z)

    loads = [
        pltpu.make_async_copy(src, dst, w_sem.at[i])
        for i, (src, dst) in enumerate(((wg_in, wg), (wu_in, wu), (wd_in, wd)))
    ]
    for load in loads:
        load.start()

    barrier = pltpu.get_barrier_semaphore()

    def greet(**peer):
        pl.semaphore_signal(barrier, inc=1, device_id=peer, device_id_type=MESH)

    greet(expert=block_at(z, 1 - y, c))
    greet(expert=block_at(z, y, 1 - c))
    greet(segment=other_segment)
    pl.when(z < n_z - 1)(lambda: greet(expert=block_at(z + 1, y, c)))
    pl.when(z > 0)(lambda: greet(expert=block_at(z - 1, y, c)))

    def block(stage, index, p):
        if stage == 0:
            return s_rows.at[index, rows_of(p)]
        return e_rows.at[stage - 1, index, rows_of(p)]

    def remote(ref, send, recv, **peer):
        return pltpu.make_async_remote_copy(
            src_ref=ref, dst_ref=ref, send_sem=send, recv_sem=recv, device_id=peer, device_id_type=MESH
        )

    def z_copy(stage, plane, way, p):
        return remote(
            block(stage, block_at(plane, y, c), p),
            z_send.at[stage, plane, way, p],
            z_recv.at[stage, plane, p],
            expert=block_at(z + 1 - 2 * way, y, c),
        )

    def y_copy(stage, plane, p, column):
        return remote(
            block(stage, block_at(plane, column, c), p),
            y_send.at[stage, plane, p],
            y_recv.at[stage, plane, p],
            expert=block_at(z, 1 - y, c),
        )

    def p_copy(stage, plane, column, p, core):
        return remote(
            block(stage, block_at(plane, column, core), p),
            p_send.at[stage, plane, column, p],
            p_recv.at[stage, plane, column, p],
            expert=block_at(z, y, 1 - c),
        )

    def send_own(stage, p):
        y_copy(stage, z, p, y).start()
        pl.when(z < n_z - 1)(lambda: z_copy(stage, z, 0, p).start())
        pl.when(z > 0)(lambda: z_copy(stage, z, 1, p).start())
        p_copy(stage, z, y, p, c).start()

    def arrivals(stage, distance):
        for p in range(PIECES):
            for d in (distance, -distance):
                plane, way, onward = z + d, int(d > 0), z - d // distance

                @pl.when(ok(plane))
                def _():
                    z_copy(stage, plane, way, p).wait_recv()
                    pl.when(ok(onward))(lambda: z_copy(stage, plane, way, p).start())
                    y_copy(stage, plane, p, y).start()
                    p_copy(stage, plane, y, p, c).start()

    def plane_ready(stage, plane):
        for p in range(PIECES):
            y_copy(stage, plane, p, 1 - y).wait_recv()
            p_copy(stage, plane, 1 - y, p, c).start()
        for column in range(2):
            for p in range(PIECES):
                p_copy(stage, plane, column, p, 1 - c).wait_recv()

    def drain_gather(stage):
        for p in range(PIECES):
            for i in range(n_z):
                y_copy(stage, i, p, y).wait_send()
                for column in range(2):
                    p_copy(stage, i, column, p, c).wait_send()
            pl.when(z < n_z - 1)(lambda: z_copy(stage, z, 0, p).wait_send())
            pl.when(z > 0)(lambda: z_copy(stage, z, 1, p).wait_send())
            for distance in range(1, n_z):
                for d in (distance, -distance):
                    plane, way, onward = z + d, int(d > 0), z - d // distance
                    pl.when(ok(plane) & ok(onward))(
                        lambda: z_copy(stage, plane, way, p).wait_send()
                    )

    def plane_of(plane):
        return pl.ds(plane * 4, 4)

    def gates_of(plane, offset):
        info = s_rows[plane_of(plane), :, width : width + INFO].reshape(plane_rows, INFO)
        info = info.astype(jnp.float32)
        route = info[:, offset : offset + top_count]
        codes = info[:, offset + top_count : offset + 2 * top_count]
        mine = jnp.where(route == me.astype(jnp.float32), codes, 0.0)
        return jnp.sum(mine, axis=-1, keepdims=True) / jnp.sum(codes, axis=-1, keepdims=True)

    strips = [pl.ds(i, STRIP) for i in range(0, hidden, STRIP)]
    wide = [pl.ds(i, 2 * STRIP) for i in range(0, width, 2 * STRIP)]

    def widen(plane):
        rows = s_rows[plane_of(plane), :, 0:width].reshape(plane_rows, width)
        for strip in strips:
            kept_g[plane, :, strip] = jnp.dot(
                rows, wg[:, strip], preferred_element_type=jnp.float32
            )
            kept_u[plane, :, strip] = jnp.dot(
                rows, wu[:, strip], preferred_element_type=jnp.float32
            )

    def keep(plane, columns, value):
        partial[plane_of(plane), :, columns] = value.astype(jnp.bfloat16).reshape(
            4, tokens, value.shape[-1]
        )

    def forward(phase, plane):
        rows = e_rows[phase, plane_of(plane)].reshape(plane_rows, width)
        coef = gates_of(plane, 0)
        for strip in strips:
            gate_part = jnp.dot(rows, wg[:, strip], preferred_element_type=jnp.float32)
            up_part = jnp.dot(rows, wu[:, strip], preferred_element_type=jnp.float32)
            mid_a[:, strip] = (gate_part * jax.nn.sigmoid(gate_part) * up_part * coef).astype(
                jnp.bfloat16
            )
        for columns in wide:
            keep(
                plane,
                columns,
                jnp.dot(mid_a[...], wd[:, columns], preferred_element_type=jnp.float32),
            )

    def backward(phase, plane):
        rows = e_rows[phase, plane_of(plane)].reshape(plane_rows, width)
        coef = gates_of(plane, 2 * top_count)
        for strip in strips:
            hidden_grad = transposed(rows, wd[strip, :]) * coef
            gate_part, up_part = kept_g[plane, :, strip], kept_u[plane, :, strip]
            sigmoid_part = jax.nn.sigmoid(gate_part)
            slope = sigmoid_part * (1.0 + gate_part * (1.0 - sigmoid_part))
            mid_a[:, strip] = (hidden_grad * up_part * slope).astype(jnp.bfloat16)
            mid_b[:, strip] = (hidden_grad * gate_part * sigmoid_part).astype(jnp.bfloat16)
        for columns in wide:
            keep(
                plane,
                columns,
                transposed(mid_a[...], wg[columns, :]) + transposed(mid_b[...], wu[columns, :]),
            )

    def q_copy(plane, column):
        return pltpu.make_async_remote_copy(
            src_ref=partial.at[block_at(plane, column, 1 - c)],
            dst_ref=paired.at[plane, column],
            send_sem=q_send.at[plane, column],
            recv_sem=q_recv.at[plane, column],
            device_id={"expert": block_at(z, y, 1 - c)},
            device_id_type=MESH,
        )

    def s_copy(plane, p):
        return pltpu.make_async_remote_copy(
            src_ref=acc.at[plane, 1 - y, rows_of(p)],
            dst_ref=crossed.at[plane, rows_of(p)],
            send_sem=s_send.at[plane, p],
            recv_sem=s_recv.at[plane, p],
            device_id={"expert": block_at(z, 1 - y, c)},
            device_id_type=MESH,
        )

    def c_copy(way, plane, p):
        return pltpu.make_async_remote_copy(
            src_ref=acc.at[plane, y, rows_of(p)],
            dst_ref=chained.at[way, plane, rows_of(p)],
            send_sem=c_send.at[plane, p],
            recv_sem=c_recv.at[way, plane, p],
            device_id={"expert": block_at(z + 1 - 2 * way, y, c)},
            device_id_type=MESH,
        )

    def start_pair(plane):
        for column in range(2):
            q_copy(plane, column).start()

    def chip_sum(plane):
        for column in (1 - y, y):
            q_copy(plane, column).wait_recv()
            mine = partial[block_at(plane, column, c)].astype(jnp.float32)
            acc[plane, column] = (mine + paired[plane, column].astype(jnp.float32)).astype(acc.dtype)

    def start_side(plane):
        for p in range(PIECES):
            s_copy(plane, p).start()

    def take_side(plane, p):
        s_copy(plane, p).wait_recv()
        rows = rows_of(p)
        return acc[plane, y, rows].astype(jnp.float32) + crossed[plane, rows].astype(jnp.float32)

    def pass_on(plane, between):
        way = (plane < z).astype(jnp.int32)
        has_source = jnp.where(plane > z, z, n_z - 1 - z) > 0
        for p in range(PIECES):
            rows = rows_of(p)
            acc[plane, y, rows] = take_side(plane, p).astype(acc.dtype)
            if p == 0:
                between()

            @pl.when(has_source)
            def _():
                c_copy(way, plane, p).wait_recv()
                acc[plane, y, rows] = (
                    acc[plane, y, rows].astype(jnp.float32)
                    + chained[way, plane, rows].astype(jnp.float32)
                ).astype(acc.dtype)

            c_copy(way, plane, p).start()

    def finish_piece(forward_flag, base, p):
        rows = rows_of(p)
        summed = take_side(z, p)
        for way, there in ((0, z > 0), (1, z < n_z - 1)):
            pl.when(there)(lambda: c_copy(way, z, p).wait_recv())
            summed = summed + jnp.where(there, chained[way, z, rows].astype(jnp.float32), 0.0)
        base_rows = base[rows].astype(jnp.float32)
        stored = stored_ref[rows].astype(jnp.float32)
        scaling = rms_scale(stored)
        scaled = summed * gain_ref[...]
        inner = jnp.mean(scaled * stored, axis=-1, keepdims=True)
        change = scaling * scaled - stored * (scaling * scaling * scaling * inner)
        return (base_rows + jnp.where(forward_flag, summed, change)).astype(jnp.bfloat16)

    def entering(forward_flag, rows):
        wide_rows = rows.astype(jnp.float32)
        normed = wide_rows * rms_scale(wide_rows) * gain_ref[...]
        return jnp.where(forward_flag, normed, wide_rows).astype(jnp.bfloat16)

    def x_copy(p):
        return pltpu.make_async_remote_copy(
            src_ref=produced.at[rows_of(p)],
            dst_ref=base_next.at[rows_of(p)],
            send_sem=x_send.at[p],
            recv_sem=x_recv.at[p],
            device_id={"segment": other_segment},
            device_id_type=MESH,
        )

    def run_phase(phase, forward_flag, finishing):
        stage = phase + 1

        def compute(plane):
            pl.when(forward_flag)(lambda: forward(phase, plane))
            pl.when(jnp.logical_not(forward_flag))(lambda: backward(phase, plane))
            start_pair(plane)

        for i in range(n_z):
            if i < n_z - 1:
                arrivals(stage, i + 1)
            plane_ready(stage, order[i])
            compute(order[i])
            if i == n_z - 2:
                chip_sum(order[i])
                start_side(order[i])
                for near in range(n_z - 2):
                    chip_sum(order[near])
        chip_sum(order[n_z - 1])
        start_side(order[n_z - 1])
        for i in range(n_z - 1, 0, -1):

            def between():
                if i == n_z - 1:
                    start_side(order[n_z - 3])
                elif i <= n_z - 3:
                    start_side(order[i - 1])

            pass_on(order[i], between)
        for p in range(PIECES):
            finishing(p)
        for i in range(n_z):
            for column in range(2):
                q_copy(i, column).wait_send()
            for p in range(PIECES):
                s_copy(i, p).wait_send()
        for i in range(1, n_z):
            for p in range(PIECES):
                c_copy((order[i] < z).astype(jnp.int32), order[i], p).wait_send()

    own = block_at(z, y, c)
    s_rows[own, :, 0:width] = entering(True, stored_ref[...])
    lists = [ref[b].astype(jnp.float32) for b in range(2) for ref in (route_ref, code_ref)]
    lists.append(jnp.zeros((INFO - 4 * top_count, tokens), jnp.float32))
    s_rows[own, :, width : width + INFO] = jnp.concatenate(lists, axis=0).T.astype(jnp.bfloat16)
    pl.semaphore_wait(barrier, 3 + jnp.minimum(z, 1) + jnp.minimum(n_z - 1 - z, 1))
    for p in range(PIECES):
        send_own(0, p)
    e_rows[0, own] = entering(first, edge_ref[...])
    for i in range(n_z):
        if i < n_z - 1:
            arrivals(0, i + 1)
        if i == n_z - 2:
            for p in range(PIECES):
                send_own(1, p)
        plane_ready(0, order[i])
        if i == 0:
            loads[0].wait()
            loads[1].wait()
        widen(order[i])
    loads[2].wait()

    def hand_over(p):
        produced[rows_of(p)] = finish_piece(first, edge_ref, p)
        x_copy(p).start()

    run_phase(0, first, hand_over)
    for p in range(PIECES):
        rows = rows_of(p)
        x_copy(p).wait_recv()
        e_rows[1, own, rows] = entering(jnp.logical_not(first), base_next[rows])
        send_own(2, p)

    def deliver(p):
        out_ref[rows_of(p)] = finish_piece(jnp.logical_not(first), base_next, p)

    run_phase(1, jnp.logical_not(first), deliver)
    for p in range(PIECES):
        x_copy(p).wait_send()
    for stage in range(3):
        drain_gather(stage)


def dense_body(boundary, saved, norm_gain, gate_weight, up_weight, down_weight, routes, gate_codes):
    n_peer = lax.axis_size("expert")
    n_z = n_peer // 4
    tokens, width = boundary.shape[1:]
    hidden = gate_weight.shape[-1]
    top_count = routes.shape[-1]
    kind, total = jnp.bfloat16, jnp.float32
    dma = pltpu.SemaphoreType.DMA
    result = pl.pallas_call(
        functools.partial(section_kernel, n_peer, top_count),
        out_shape=jax.ShapeDtypeStruct((tokens, width), kind),
        in_specs=[pl.BlockSpec(memory_space=pltpu.VMEM)] * 5
        + [pl.BlockSpec(memory_space=pl.ANY)] * 3,
        out_specs=pl.BlockSpec(memory_space=pltpu.VMEM),
        scratch_shapes=[
            pltpu.VMEM((n_peer, tokens, width + INFO), kind),
            pltpu.VMEM((2, n_peer, tokens, width), kind),
            pltpu.VMEM((width, hidden), kind),
            pltpu.VMEM((width, hidden), kind),
            pltpu.VMEM((hidden, width), kind),
            pltpu.VMEM((n_z, 4 * tokens, hidden), total),
            pltpu.VMEM((n_z, 4 * tokens, hidden), total),
            pltpu.VMEM((4 * tokens, hidden), kind),
            pltpu.VMEM((4 * tokens, hidden), kind),
            pltpu.VMEM((n_peer, tokens, width), kind),
            pltpu.VMEM((n_z, 2, tokens, width), kind),
            pltpu.VMEM((n_z, 2, tokens, width), kind),
            pltpu.VMEM((n_z, tokens, width), kind),
            pltpu.VMEM((2, n_z, tokens, width), kind),
            pltpu.VMEM((tokens, width), kind),
            pltpu.VMEM((tokens, width), kind),
            dma((3,)),
            dma((3, n_z, 2, PIECES)),
            dma((3, n_z, PIECES)),
            dma((3, n_z, PIECES)),
            dma((3, n_z, PIECES)),
            dma((3, n_z, 2, PIECES)),
            dma((3, n_z, 2, PIECES)),
            dma((n_z, 2)),
            dma((n_z, 2)),
            dma((n_z, PIECES)),
            dma((n_z, PIECES)),
            dma((n_z, PIECES)),
            dma((2, n_z, PIECES)),
            dma((PIECES,)),
            dma((PIECES,)),
        ],
        compiler_params=pltpu.CompilerParams(
            collective_id=1, has_side_effects=True, vmem_limit_bytes=60 << 20
        ),
        cost_estimate=pl.CostEstimate(
            flops=2 * n_peer * tokens * width * hidden * 8,
            bytes_accessed=6 * width * hidden,
            transcendentals=0,
        ),
        name="two_sections",
    )(
        boundary[0],
        saved[0],
        norm_gain,
        routes[0].swapaxes(1, 2),
        gate_codes[0].swapaxes(1, 2),
        gate_weight[0, 0],
        up_weight[0, 0],
        down_weight[0, 0],
    )
    return result[None]


def body(*arrays):
    tokens, top_count = arrays[0].shape[1], arrays[6].shape[3]
    n_peer = lax.axis_size("expert")
    capacity = max(2, 3 * tokens * top_count // (2 * n_peer))
    planes = n_peer % 4 == 0 and n_peer >= 12 and lax.axis_size("segment") == 2
    chosen = dense_body if tokens <= 2 * capacity and planes else routed_body
    return chosen(*arrays)


def solution(mesh):
    return jax.shard_map(
        body,
        mesh=mesh,
        in_specs=(
            P("segment", "expert", None),
            P("segment", "expert", None),
            P("segment", None),
            P("segment", "expert", None, None),
            P("segment", "expert", None, None),
            P("segment", "expert", None, None),
            P("segment", None, "expert", None),
            P("segment", None, "expert", None),
        ),
        out_specs=P("segment", "expert", None),
        check_vma=False,
    )
```

```python
import functools

import jax
import jax.numpy as jnp
from jax import lax
from jax.experimental import pallas as pl
from jax.experimental.pallas import tpu as pltpu
from jax.sharding import PartitionSpec as P

epsilon = 1e-06


def shifted(block, axis, distance):
    devices = range(lax.axis_size(axis))
    route = [(i - distance, i) for i in devices if i - distance in devices]
    return lax.ppermute(block, axis, route)


def gate_values(codes):
    counted = codes.astype(jnp.float32)
    return counted / jnp.sum(counted, axis=-1, keepdims=True)


def normalize(inputs, gain_row):
    widened = inputs.astype(jnp.float32)
    scaling = lax.rsqrt(jnp.mean(widened * widened, axis=-1, keepdims=True) + epsilon)
    return (widened, scaling, (widened * scaling * gain_row).astype(jnp.bfloat16))


def transposed(left, right):
    return lax.dot_general(
        left, right, (((1,), (1,)), ((), ())), preferred_element_type=jnp.float32
    )


def expert_forward(row_block, w_gate, w_up, w_down):
    gate_part = jnp.dot(row_block, w_gate, preferred_element_type=jnp.float32)
    up_part = jnp.dot(row_block, w_up, preferred_element_type=jnp.float32)
    hidden = (gate_part * jax.nn.sigmoid(gate_part) * up_part).astype(jnp.bfloat16)
    return jnp.dot(hidden, w_down, preferred_element_type=jnp.float32).astype(jnp.bfloat16)


def expert_backward(row_block, grad_block, w_gate, w_up, w_down):
    gate_part = jnp.dot(row_block, w_gate, preferred_element_type=jnp.float32)
    up_part = jnp.dot(row_block, w_up, preferred_element_type=jnp.float32)
    sigmoid_part = jax.nn.sigmoid(gate_part)
    activated = gate_part * sigmoid_part
    slope = sigmoid_part * (1.0 + gate_part * (1.0 - sigmoid_part))
    hidden_grad = transposed(grad_block, w_down)
    gate_grad = (hidden_grad * up_part * slope).astype(jnp.bfloat16)
    up_grad = (hidden_grad * activated).astype(jnp.bfloat16)
    return (transposed(gate_grad, w_gate) + transposed(up_grad, w_up)).astype(jnp.bfloat16)


def layout(route, codes, n_peer, capacity):
    tokens, top_count = route.shape
    flat_ids = route.reshape(-1)
    onehot = (flat_ids[:, None] == jnp.arange(n_peer, dtype=jnp.int32)[None, :]).astype(jnp.int32)
    spots = jnp.arange(flat_ids.shape[0], dtype=jnp.int32)
    earlier = (spots[None, :] < spots[:, None]).astype(jnp.bfloat16)
    before = jnp.dot(earlier, onehot.astype(jnp.bfloat16), preferred_element_type=jnp.float32)
    rank_in = jnp.sum(before.astype(jnp.int32) * onehot, axis=1)
    slot_of = flat_ids * capacity + rank_in
    slot_ids = jnp.arange(n_peer * capacity, dtype=jnp.int32)
    slot_hit = (slot_ids[:, None, None] == slot_of.reshape(tokens, top_count)[None, :, :]).astype(
        jnp.bfloat16
    )
    placing = jnp.sum(slot_hit, axis=2, dtype=jnp.float32).astype(jnp.bfloat16)
    return (placing, slot_of, gate_values(codes))


def dispatch(placing, payload, n_peer, capacity):
    picked = jnp.dot(placing, payload, preferred_element_type=jnp.float32).astype(jnp.bfloat16)
    return picked.reshape(n_peer, capacity, payload.shape[-1])


def collect(slot_of, gates, came_back):
    flat_rows = came_back.reshape(-1, came_back.shape[-1])
    chosen = jnp.take(flat_rows, slot_of, axis=0).reshape(
        gates.shape[0], gates.shape[1], flat_rows.shape[-1]
    )
    return jnp.einsum("tk,tkd->td", gates, chosen.astype(jnp.float32))


def apply_expert(forward_flag, first_rows, second_rows, weights):
    layout_of = first_rows.shape
    row_block = first_rows.reshape(-1, layout_of[-1])
    grad_block = second_rows.reshape(-1, layout_of[-1])
    outcome = lax.cond(
        forward_flag,
        lambda: expert_forward(row_block, weights[0], weights[1], weights[2]),
        lambda: expert_backward(row_block, grad_block, weights[0], weights[1], weights[2]),
    )
    return outcome.reshape(layout_of)


def return_rows(outcome):
    return lax.all_to_all(outcome, "expert", split_axis=0, concat_axis=0, tiled=True)


def finish(widened, scaling, gain_row, upstream, summed, forward_flag):
    forward_out = widened + summed
    scaled = summed * gain_row
    inner_mean = jnp.mean(scaled * widened, axis=-1, keepdims=True)
    cubed = scaling * scaling * scaling
    backward_out = upstream.astype(jnp.float32) + scaling * scaled - widened * cubed * inner_mean
    return jnp.where(forward_flag, forward_out, backward_out).astype(jnp.bfloat16)


def routed_body(boundary, saved, norm_gain, gate_weight, up_weight, down_weight, routes, gate_codes):
    first_segment = lax.axis_index("segment") == 0
    later_forward = jnp.logical_not(first_segment)
    n_peer = lax.axis_size("expert")
    tokens = boundary.shape[1]
    top_count = routes.shape[3]
    capacity = max(2, 3 * tokens * top_count // (2 * n_peer))
    weights = (gate_weight[0, 0], up_weight[0, 0], down_weight[0, 0])
    gain_row = norm_gain[0]
    edge_rows = boundary[0]
    stored = saved[0]
    route_now = jnp.where(first_segment, routes[0, 0], routes[0, 1])
    codes_now = jnp.where(first_segment, gate_codes[0, 0], gate_codes[0, 1])
    route_next = jnp.where(first_segment, routes[0, 1], routes[0, 0])
    codes_next = jnp.where(first_segment, gate_codes[0, 1], gate_codes[0, 0])
    place_now, slots_now, gates_now = layout(route_now, codes_now, n_peer, capacity)
    place_next, slots_next, gates_next = layout(route_next, codes_next, n_peer, capacity)
    inputs_now = jnp.where(first_segment, edge_rows, stored)
    widened, scaling, normed = normalize(inputs_now, gain_row)
    stored_normed = normalize(stored, gain_row)[2]
    early_rows = jnp.where(first_segment, stored_normed, edge_rows)
    early_place = jnp.where(first_segment, place_next, place_now)
    outgoing = (
        dispatch(place_now, normed, n_peer, capacity),
        dispatch(early_place, early_rows, n_peer, capacity),
    )
    paired = (
        lax.all_to_all(outgoing[0], "expert", split_axis=0, concat_axis=0, tiled=True),
        lax.all_to_all(outgoing[1], "expert", split_axis=0, concat_axis=0, tiled=True),
    )
    outcome = apply_expert(first_segment, paired[0], paired[1], weights)
    came_back = return_rows(outcome)
    kept_rows = paired[1]
    produced = finish(
        widened,
        scaling,
        gain_row,
        edge_rows,
        collect(slots_now, gates_now, came_back),
        first_segment,
    )
    arrived = shifted(produced, "segment", 1) + shifted(produced, "segment", -1)
    inputs_next = jnp.where(first_segment, stored, arrived)
    widened_next, scaling_next, normed_next = normalize(inputs_next, gain_row)
    member = jnp.where(first_segment, arrived, normed_next)
    landed = lax.all_to_all(
        dispatch(place_next, member, n_peer, capacity),
        "expert",
        split_axis=0,
        concat_axis=0,
        tiled=True,
    )
    outcome = apply_expert(
        later_forward, jnp.where(first_segment, kept_rows, landed), landed, weights
    )
    came_next = return_rows(outcome)
    result = finish(
        widened_next,
        scaling_next,
        gain_row,
        arrived,
        collect(slots_next, gates_next, came_next),
        later_forward,
    )
    return result[None]


PIECES = 2
INFO = 128
STRIP = 256
MESH = pl.DeviceIdType.MESH


def position(n_peer):
    me = lax.axis_index("expert")
    return me, me // 4, me // 2 % 2, me % 2, n_peer // 4


def block_at(z, y, c):
    return (z * 2 + y) * 2 + c


def nearest_first(z, n_z):
    tables = []
    for at in range(n_z):
        inward = 1 if 2 * at < n_z else -1
        steps = [0] + [s * d for d in range(1, n_z) for s in (inward, -inward)]
        tables.append([at + s for s in steps if 0 <= at + s < n_z])
    order = []
    for i in range(n_z):
        chosen = jnp.int32(tables[0][i])
        for at in range(1, n_z):
            chosen = jnp.where(z == at, jnp.int32(tables[at][i]), chosen)
        order.append(chosen)
    return order


def rms_scale(rows):
    return lax.rsqrt(jnp.mean(rows * rows, axis=-1, keepdims=True) + epsilon)


def section_kernel(n_peer, top_count, *refs):
    edge_ref, stored_ref, gain_ref, route_ref, code_ref, wg_in, wu_in, wd_in, out_ref = refs[:9]
    refs = refs[1:]
    s_rows, e_rows, wg, wu, wd, kept_g, kept_u, mid_a, mid_b = refs[8:17]
    partial, paired, acc, crossed, chained, base_next, produced = refs[17:24]
    w_sem, z_send, z_recv, y_send, y_recv, p_send, p_recv = refs[24:31]
    q_send, q_recv, s_send, s_recv, c_send, c_recv, x_send, x_recv = refs[31:]
    first = lax.axis_index("segment") == 0
    other_segment = 1 - lax.axis_index("segment")
    me, z, y, c, n_z = position(n_peer)
    tokens, width = edge_ref.shape
    hidden = wg.shape[1]
    plane_rows = 4 * tokens
    piece = tokens // PIECES
    order = nearest_first(z, n_z)

    def rows_of(p):
        return pl.ds(p * piece, piece)

    def ok(plane):
        return (plane >= 0) & (plane < n_z)

    loads = [
        pltpu.make_async_copy(src, dst, w_sem.at[i])
        for i, (src, dst) in enumerate(((wg_in, wg), (wu_in, wu), (wd_in, wd)))
    ]
    for load in loads:
        load.start()

    barrier = pltpu.get_barrier_semaphore()

    def greet(**peer):
        pl.semaphore_signal(barrier, inc=1, device_id=peer, device_id_type=MESH)

    greet(expert=block_at(z, 1 - y, c))
    greet(expert=block_at(z, y, 1 - c))
    greet(segment=other_segment)
    pl.when(z < n_z - 1)(lambda: greet(expert=block_at(z + 1, y, c)))
    pl.when(z > 0)(lambda: greet(expert=block_at(z - 1, y, c)))

    def block(stage, index, p):
        if stage == 0:
            return s_rows.at[index, rows_of(p)]
        return e_rows.at[stage - 1, index, rows_of(p)]

    def remote(ref, send, recv, **peer):
        return pltpu.make_async_remote_copy(
            src_ref=ref, dst_ref=ref, send_sem=send, recv_sem=recv, device_id=peer, device_id_type=MESH
        )

    def z_copy(stage, plane, way, p):
        return remote(
            block(stage, block_at(plane, y, c), p),
            z_send.at[stage, plane, way, p],
            z_recv.at[stage, plane, p],
            expert=block_at(z + 1 - 2 * way, y, c),
        )

    def y_copy(stage, plane, p, column):
        return remote(
            block(stage, block_at(plane, column, c), p),
            y_send.at[stage, plane, p],
            y_recv.at[stage, plane, p],
            expert=block_at(z, 1 - y, c),
        )

    def p_copy(stage, plane, column, p, core):
        return remote(
            block(stage, block_at(plane, column, core), p),
            p_send.at[stage, plane, column, p],
            p_recv.at[stage, plane, column, p],
            expert=block_at(z, y, 1 - c),
        )

    def send_own(stage, p):
        y_copy(stage, z, p, y).start()
        pl.when(z < n_z - 1)(lambda: z_copy(stage, z, 0, p).start())
        pl.when(z > 0)(lambda: z_copy(stage, z, 1, p).start())
        p_copy(stage, z, y, p, c).start()

    def arrivals(stage, distance):
        for p in range(PIECES):
            for d in (distance, -distance):
                plane, way, onward = z + d, int(d > 0), z - d // distance

                @pl.when(ok(plane))
                def _():
                    z_copy(stage, plane, way, p).wait_recv()
                    pl.when(ok(onward))(lambda: z_copy(stage, plane, way, p).start())
                    y_copy(stage, plane, p, y).start()
                    p_copy(stage, plane, y, p, c).start()

    def plane_ready(stage, plane):
        for p in range(PIECES):
            y_copy(stage, plane, p, 1 - y).wait_recv()
            p_copy(stage, plane, 1 - y, p, c).start()
        for column in range(2):
            for p in range(PIECES):
                p_copy(stage, plane, column, p, 1 - c).wait_recv()

    def drain_gather(stage):
        for p in range(PIECES):
            for i in range(n_z):
                y_copy(stage, i, p, y).wait_send()
                for column in range(2):
                    p_copy(stage, i, column, p, c).wait_send()
            pl.when(z < n_z - 1)(lambda: z_copy(stage, z, 0, p).wait_send())
            pl.when(z > 0)(lambda: z_copy(stage, z, 1, p).wait_send())
            for distance in range(1, n_z):
                for d in (distance, -distance):
                    plane, way, onward = z + d, int(d > 0), z - d // distance
                    pl.when(ok(plane) & ok(onward))(
                        lambda: z_copy(stage, plane, way, p).wait_send()
                    )

    def plane_of(plane):
        return pl.ds(plane * 4, 4)

    def gates_of(plane, offset):
        info = s_rows[plane_of(plane), :, width : width + INFO].reshape(plane_rows, INFO)
        info = info.astype(jnp.float32)
        route = info[:, offset : offset + top_count]
        codes = info[:, offset + top_count : offset + 2 * top_count]
        mine = jnp.where(route == me.astype(jnp.float32), codes, 0.0)
        return jnp.sum(mine, axis=-1, keepdims=True) / jnp.sum(codes, axis=-1, keepdims=True)

    strips = [pl.ds(i, STRIP) for i in range(0, hidden, STRIP)]
    wide = [pl.ds(i, 2 * STRIP) for i in range(0, width, 2 * STRIP)]

    def widen(plane):
        rows = s_rows[plane_of(plane), :, 0:width].reshape(plane_rows, width)
        for strip in strips:
            kept_g[plane, :, strip] = jnp.dot(
                rows, wg[:, strip], preferred_element_type=jnp.float32
            )
            kept_u[plane, :, strip] = jnp.dot(
                rows, wu[:, strip], preferred_element_type=jnp.float32
            )

    def keep(plane, columns, value):
        partial[plane_of(plane), :, columns] = value.astype(jnp.bfloat16).reshape(
            4, tokens, value.shape[-1]
        )

    def forward(phase, plane):
        rows = e_rows[phase, plane_of(plane)].reshape(plane_rows, width)
        coef = gates_of(plane, 0)
        for strip in strips:
            gate_part = jnp.dot(rows, wg[:, strip], preferred_element_type=jnp.float32)
            up_part = jnp.dot(rows, wu[:, strip], preferred_element_type=jnp.float32)
            mid_a[:, strip] = (gate_part * jax.nn.sigmoid(gate_part) * up_part * coef).astype(
                jnp.bfloat16
            )
        for columns in wide:
            keep(
                plane,
                columns,
                jnp.dot(mid_a[...], wd[:, columns], preferred_element_type=jnp.float32),
            )

    def backward(phase, plane):
        rows = e_rows[phase, plane_of(plane)].reshape(plane_rows, width)
        coef = gates_of(plane, 2 * top_count)
        for strip in strips:
            hidden_grad = transposed(rows, wd[strip, :]) * coef
            gate_part, up_part = kept_g[plane, :, strip], kept_u[plane, :, strip]
            sigmoid_part = jax.nn.sigmoid(gate_part)
            slope = sigmoid_part * (1.0 + gate_part * (1.0 - sigmoid_part))
            mid_a[:, strip] = (hidden_grad * up_part * slope).astype(jnp.bfloat16)
            mid_b[:, strip] = (hidden_grad * gate_part * sigmoid_part).astype(jnp.bfloat16)
        for columns in wide:
            keep(
                plane,
                columns,
                transposed(mid_a[...], wg[columns, :]) + transposed(mid_b[...], wu[columns, :]),
            )

    def q_copy(plane, column):
        return pltpu.make_async_remote_copy(
            src_ref=partial.at[block_at(plane, column, 1 - c)],
            dst_ref=paired.at[plane, column],
            send_sem=q_send.at[plane, column],
            recv_sem=q_recv.at[plane, column],
            device_id={"expert": block_at(z, y, 1 - c)},
            device_id_type=MESH,
        )

    def s_copy(plane, p):
        return pltpu.make_async_remote_copy(
            src_ref=acc.at[plane, 1 - y, rows_of(p)],
            dst_ref=crossed.at[plane, rows_of(p)],
            send_sem=s_send.at[plane, p],
            recv_sem=s_recv.at[plane, p],
            device_id={"expert": block_at(z, 1 - y, c)},
            device_id_type=MESH,
        )

    def c_copy(way, plane, p):
        return pltpu.make_async_remote_copy(
            src_ref=acc.at[plane, y, rows_of(p)],
            dst_ref=chained.at[way, plane, rows_of(p)],
            send_sem=c_send.at[plane, p],
            recv_sem=c_recv.at[way, plane, p],
            device_id={"expert": block_at(z + 1 - 2 * way, y, c)},
            device_id_type=MESH,
        )

    def start_pair(plane):
        for column in range(2):
            q_copy(plane, column).start()

    def chip_sum(plane):
        for column in (1 - y, y):
            q_copy(plane, column).wait_recv()
            mine = partial[block_at(plane, column, c)].astype(jnp.float32)
            acc[plane, column] = (mine + paired[plane, column].astype(jnp.float32)).astype(acc.dtype)

    def start_side(plane):
        for p in range(PIECES):
            s_copy(plane, p).start()

    def take_side(plane, p):
        s_copy(plane, p).wait_recv()
        rows = rows_of(p)
        return acc[plane, y, rows].astype(jnp.float32) + crossed[plane, rows].astype(jnp.float32)

    def pass_on(plane):
        way = (plane < z).astype(jnp.int32)
        has_source = jnp.where(plane > z, z, n_z - 1 - z) > 0
        for p in range(PIECES):
            rows = rows_of(p)
            acc[plane, y, rows] = take_side(plane, p).astype(acc.dtype)

            @pl.when(has_source)
            def _():
                c_copy(way, plane, p).wait_recv()
                acc[plane, y, rows] = (
                    acc[plane, y, rows].astype(jnp.float32)
                    + chained[way, plane, rows].astype(jnp.float32)
                ).astype(acc.dtype)

            c_copy(way, plane, p).start()

    def finish_piece(forward_flag, base, p):
        rows = rows_of(p)
        summed = take_side(z, p)
        for way, there in ((0, z > 0), (1, z < n_z - 1)):
            pl.when(there)(lambda: c_copy(way, z, p).wait_recv())
            summed = summed + jnp.where(there, chained[way, z, rows].astype(jnp.float32), 0.0)
        base_rows = base[rows].astype(jnp.float32)
        stored = stored_ref[rows].astype(jnp.float32)
        scaling = rms_scale(stored)
        scaled = summed * gain_ref[...]
        inner = jnp.mean(scaled * stored, axis=-1, keepdims=True)
        change = scaling * scaled - stored * (scaling * scaling * scaling * inner)
        return (base_rows + jnp.where(forward_flag, summed, change)).astype(jnp.bfloat16)

    def entering(forward_flag, rows):
        wide_rows = rows.astype(jnp.float32)
        normed = wide_rows * rms_scale(wide_rows) * gain_ref[...]
        return jnp.where(forward_flag, normed, wide_rows).astype(jnp.bfloat16)

    def x_copy(p):
        return pltpu.make_async_remote_copy(
            src_ref=produced.at[rows_of(p)],
            dst_ref=base_next.at[rows_of(p)],
            send_sem=x_send.at[p],
            recv_sem=x_recv.at[p],
            device_id={"segment": other_segment},
            device_id_type=MESH,
        )

    def run_phase(phase, forward_flag, finishing):
        stage = phase + 1

        def compute(plane):
            pl.when(forward_flag)(lambda: forward(phase, plane))
            pl.when(jnp.logical_not(forward_flag))(lambda: backward(phase, plane))
            start_pair(plane)

        for i in range(n_z):
            if i < n_z - 1:
                arrivals(stage, i + 1)
            plane_ready(stage, order[i])
            compute(order[i])
            if i == n_z - 2:
                chip_sum(order[i])
                start_side(order[i])
                for near in range(n_z - 2):
                    chip_sum(order[near])
        chip_sum(order[n_z - 1])
        start_side(order[n_z - 1])
        for i in range(n_z - 3, -1, -1):
            start_side(order[i])
        for i in range(n_z - 1, 0, -1):
            pass_on(order[i])
        for p in range(PIECES):
            finishing(p)
        for i in range(n_z):
            for column in range(2):
                q_copy(i, column).wait_send()
            for p in range(PIECES):
                s_copy(i, p).wait_send()
        for i in range(1, n_z):
            for p in range(PIECES):
                c_copy((order[i] < z).astype(jnp.int32), order[i], p).wait_send()

    own = block_at(z, y, c)
    s_rows[own, :, 0:width] = entering(True, stored_ref[...])
    lists = [ref[b].astype(jnp.float32) for b in range(2) for ref in (route_ref, code_ref)]
    lists.append(jnp.zeros((INFO - 4 * top_count, tokens), jnp.float32))
    s_rows[own, :, width : width + INFO] = jnp.concatenate(lists, axis=0).T.astype(jnp.bfloat16)
    pl.semaphore_wait(barrier, 3 + jnp.minimum(z, 1) + jnp.minimum(n_z - 1 - z, 1))
    for p in range(PIECES):
        send_own(0, p)
    e_rows[0, own] = entering(first, edge_ref[...])
    for i in range(n_z):
        if i < n_z - 1:
            arrivals(0, i + 1)
        if i == n_z - 2:
            for p in range(PIECES):
                send_own(1, p)
        plane_ready(0, order[i])
        if i == 0:
            loads[0].wait()
            loads[1].wait()
        widen(order[i])
    loads[2].wait()

    def hand_over(p):
        produced[rows_of(p)] = finish_piece(first, edge_ref, p)
        x_copy(p).start()

    run_phase(0, first, hand_over)
    for p in range(PIECES):
        rows = rows_of(p)
        x_copy(p).wait_recv()
        e_rows[1, own, rows] = entering(jnp.logical_not(first), base_next[rows])
        send_own(2, p)

    def deliver(p):
        out_ref[rows_of(p)] = finish_piece(jnp.logical_not(first), base_next, p)

    run_phase(1, jnp.logical_not(first), deliver)
    for p in range(PIECES):
        x_copy(p).wait_send()
    for stage in range(3):
        drain_gather(stage)


def dense_body(boundary, saved, norm_gain, gate_weight, up_weight, down_weight, routes, gate_codes):
    n_peer = lax.axis_size("expert")
    n_z = n_peer // 4
    tokens, width = boundary.shape[1:]
    hidden = gate_weight.shape[-1]
    top_count = routes.shape[-1]
    kind, total = jnp.bfloat16, jnp.float32
    dma = pltpu.SemaphoreType.DMA
    result = pl.pallas_call(
        functools.partial(section_kernel, n_peer, top_count),
        out_shape=jax.ShapeDtypeStruct((tokens, width), kind),
        in_specs=[pl.BlockSpec(memory_space=pltpu.VMEM)] * 5
        + [pl.BlockSpec(memory_space=pl.ANY)] * 3,
        out_specs=pl.BlockSpec(memory_space=pltpu.VMEM),
        scratch_shapes=[
            pltpu.VMEM((n_peer, tokens, width + INFO), kind),
            pltpu.VMEM((2, n_peer, tokens, width), kind),
            pltpu.VMEM((width, hidden), kind),
            pltpu.VMEM((width, hidden), kind),
            pltpu.VMEM((hidden, width), kind),
            pltpu.VMEM((n_z, 4 * tokens, hidden), total),
            pltpu.VMEM((n_z, 4 * tokens, hidden), total),
            pltpu.VMEM((4 * tokens, hidden), kind),
            pltpu.VMEM((4 * tokens, hidden), kind),
            pltpu.VMEM((n_peer, tokens, width), kind),
            pltpu.VMEM((n_z, 2, tokens, width), kind),
            pltpu.VMEM((n_z, 2, tokens, width), kind),
            pltpu.VMEM((n_z, tokens, width), kind),
            pltpu.VMEM((2, n_z, tokens, width), kind),
            pltpu.VMEM((tokens, width), kind),
            pltpu.VMEM((tokens, width), kind),
            dma((3,)),
            dma((3, n_z, 2, PIECES)),
            dma((3, n_z, PIECES)),
            dma((3, n_z, PIECES)),
            dma((3, n_z, PIECES)),
            dma((3, n_z, 2, PIECES)),
            dma((3, n_z, 2, PIECES)),
            dma((n_z, 2)),
            dma((n_z, 2)),
            dma((n_z, PIECES)),
            dma((n_z, PIECES)),
            dma((n_z, PIECES)),
            dma((2, n_z, PIECES)),
            dma((PIECES,)),
            dma((PIECES,)),
        ],
        compiler_params=pltpu.CompilerParams(
            collective_id=1, has_side_effects=True, vmem_limit_bytes=60 << 20
        ),
        cost_estimate=pl.CostEstimate(
            flops=2 * n_peer * tokens * width * hidden * 8,
            bytes_accessed=6 * width * hidden,
            transcendentals=0,
        ),
        name="two_sections",
    )(
        boundary[0],
        saved[0],
        norm_gain,
        routes[0].swapaxes(1, 2),
        gate_codes[0].swapaxes(1, 2),
        gate_weight[0, 0],
        up_weight[0, 0],
        down_weight[0, 0],
    )
    return result[None]


def body(*arrays):
    tokens, top_count = arrays[0].shape[1], arrays[6].shape[3]
    n_peer = lax.axis_size("expert")
    capacity = max(2, 3 * tokens * top_count // (2 * n_peer))
    planes = n_peer % 4 == 0 and n_peer >= 12 and lax.axis_size("segment") == 2
    chosen = dense_body if tokens <= 2 * capacity and planes else routed_body
    return chosen(*arrays)


def solution(mesh):
    return jax.shard_map(
        body,
        mesh=mesh,
        in_specs=(
            P("segment", "expert", None),
            P("segment", "expert", None),
            P("segment", None),
            P("segment", "expert", None, None),
            P("segment", "expert", None, None),
            P("segment", "expert", None, None),
            P("segment", None, "expert", None),
            P("segment", None, "expert", None),
        ),
        out_specs=P("segment", "expert", None),
        check_vma=False,
    )
```
